512 devices in a mesh: dp: 32 (over y_lo, x, core), vocab: 16 (over z, y_hi).
Axes of the slice: x: 4, y: 8 (y_hi: 2, y_lo: 4; y = y_hi * 4 + y_lo), z: 8, core: 2. Of those that a mesh axis runs over, the one named last changes fastest.
Arguments:
- logits: bfloat16 [6144, 128256], P('dp', 'vocab'), may hold values from -128 to 320
- labels: int32 [6144], P('dp'), may hold values from 0 to 128255
- hidden: bfloat16 [6144, 4096], P('dp', 'vocab'), may hold values from -6 to 6
- proj_in: bfloat16 [4096, 64], P('vocab'), may hold values from -0.09375 to 0.09375
- proj_out: bfloat16 [128256, 64], P('vocab'), may hold values from -6 to 6
- test_grads: bfloat16 [4096, 4096], P('dp', 'vocab'), may hold values from -0.01171875 to 0.01171875
- group_ids: int32 [96], P('dp'), may hold values from 0 to 31
Outputs:
- scores: float32 [96, 4096], P('vocab', 'dp')
- group_scores: float32 [32, 4096], P(None, 'dp')
The draws below stay inside these ranges and needn't reach their ends.
All inputs are finite; a program needn't handle non-finite values.
Results may differ from the reference program's by a relative error of at most 0.0053.
Values may be sent and summed in bfloat16 or wider, within the bound.
A program may use at most 64 MiB of HBM per device.

```python
import math
import jax
import jax.numpy as jnp
from jax import lax

D = 4096
VOCAB = 128256
RANK = 64
SPAN = 64
GROUPS = 32
TOKENS = 6144
SPANS = 96
TESTS = 4096


def draw_logits(key, part):
    keys = jax.random.split(key, 3)
    column = jnp.arange(VOCAB, dtype=jnp.float32)
    ramp = jnp.log1p(2.0 * column / VOCAB)[None, :]
    row_scale = jnp.exp(jax.random.uniform(keys[0], (TOKENS, 1)) * 0.5 * math.log(10.0))
    col_scale = jnp.exp(jax.random.uniform(keys[1], (1, VOCAB)) * 0.5 * math.log(10.0))
    spread = 3.0 * row_scale * col_scale
    normal = jnp.clip(jax.random.normal(keys[2], (TOKENS, VOCAB)), -4.0, 4.0)
    values = normal * spread + ramp
    return values.astype(jnp.bfloat16)


def with_ends(array, stream_key, least, high):
    shape = array.shape
    spot = [jax.random.randint(jax.random.fold_in(stream_key, axis), (), 0, shape[axis]) for axis in range(len(shape))]
    array = array.at[tuple(spot)].set(least)
    longest = shape.index(max(shape))
    spot[longest] = (spot[longest] + 1) % shape[longest]
    return array.at[tuple(spot)].set(high)


def level_of(key, shape, cuts, low, high):
    def one(axis_at, parts):
        draws = jax.random.uniform(jax.random.fold_in(jax.random.fold_in(key, 6), axis_at), (parts,), jnp.float32, low / len(cuts), high / len(cuts))
        return jnp.repeat(jnp.exp(draws), shape[axis_at] // parts).reshape((-1,) + (1,) * (len(shape) - axis_at - 1))

    level = one(*cuts[0])
    for cut in cuts[1:]:
        level = level * one(*cut)
    return level


def noise(rng, dims, scale, limit, pieces=(), held_as=jnp.bfloat16):
    level = level_of(rng, dims, pieces, -0.22, 0.18) if pieces else 1.0
    result = jax.random.normal(rng, dims, jnp.float32) * scale * level
    return jnp.minimum(jnp.maximum(result, -limit), limit).astype(held_as)


def setup_inputs(seed: int = 0) -> dict:
    splits = jax.random.split(jax.random.key(seed), 8)
    logits = draw_logits(jax.random.fold_in(splits[7], 71), 0)
    labels = with_ends(jax.random.randint(splits[1], (TOKENS,), 0, VOCAB), jax.random.fold_in(splits[1], 1), 0, VOCAB - 1).astype(jnp.int32)
    hidden = noise(splits[2], (TOKENS, D), 1.0, 6.0, ((0, 32), (1, 16)))
    proj_in = noise(splits[3], (D, RANK), D ** -0.5, 0.09375, ((0, 16),))
    proj_out = noise(splits[4], (VOCAB, RANK), 1.0, 6.0, ((0, 16),))
    test_grads = noise(splits[5], (TESTS, RANK * RANK), (SPAN * RANK * RANK) ** -0.5, 0.01171875, ((0, 32), (1, 16)))
    group_ids = with_ends(jax.random.randint(splits[6], (SPANS,), 0, GROUPS), jax.random.fold_in(splits[6], 1), 0, GROUPS - 1).astype(jnp.int32)
    return dict(logits=logits, labels=labels, hidden=hidden, proj_in=proj_in, proj_out=proj_out, test_grads=test_grads, group_ids=group_ids)


def reference(logits, labels, hidden, proj_in, proj_out, test_grads, group_ids):
    count = TOKENS // SPAN
    blocks = (logits.reshape(count, SPAN, VOCAB), labels.reshape(count, SPAN), hidden.reshape(count, SPAN, D))

    def one_span(block):
        logit_block, label_block, hidden_block = block
        values = logit_block.astype(jnp.float32)
        row_top = jnp.max(values, axis=1, keepdims=True)
        expo = jnp.exp(values - row_top)
        row_total = jnp.sum(expo, axis=1, keepdims=True)
        target = (jnp.arange(VOCAB, dtype=jnp.int32)[None, :] == label_block[:, None]).astype(jnp.float32)
        resid = (expo / row_total - target).astype(jnp.bfloat16)
        rproj = jnp.dot(resid, proj_out, preferred_element_type=jnp.float32).astype(jnp.bfloat16)
        hproj = jnp.dot(hidden_block, proj_in, preferred_element_type=jnp.float32).astype(jnp.bfloat16)
        grad = jnp.dot(hproj.T, rproj, preferred_element_type=jnp.float32).astype(jnp.bfloat16)
        return grad.reshape(RANK * RANK)

    grads = lax.map(one_span, blocks)
    scores = lax.dot_general(grads, test_grads, (((1,), (1,)), ((), ())), preferred_element_type=jnp.float32)
    member = (jnp.arange(GROUPS, dtype=jnp.int32)[:, None] == group_ids[None, :]).astype(jnp.float32)
    group_scores = jnp.dot(member, scores, precision=lax.Precision.HIGHEST)
    return scores, group_scores
```

```python
import functools

import jax
import jax.numpy as jnp
from jax import lax
from jax.experimental import pallas as pl
from jax.experimental.pallas import tpu as pltpu
from jax.sharding import PartitionSpec as P

RANK = 64
SPAN = 64
GROUPS = 32
MESH = pl.DeviceIdType.MESH
F32 = jnp.float32
BF16 = jnp.bfloat16
NT = (((1,), (1,)), ((), ()))
NZ = 8
KBLOCK = 1024


def dot(a, b):
    return jnp.dot(a, b, preferred_element_type=F32)


def dot_nt(a, b):
    return lax.dot_general(a, b, NT, preferred_element_type=F32)


def iota(shape, dim):
    return lax.broadcasted_iota(jnp.int32, shape, dim)


def kernel(
    ndp, row_chunks,
    logits, labels, hidden, pin, pout, tgrads, gids,
    out_s, out_g,
    xv, wv, lab, hid, pinv, tg,
    hs, hr, hy, hb, hall,
    ps, pr, py, st, sr, sy,
    ts, rt, tb,
    gs0, gr0, gs, gr, cmat,
    fg, fgr, fs, fsr,
    lsem, xsem,
    hr_s, hr_r, hy_s, hy_r, hb_s, hb_r,
    pr_s, pr_r, py_s, py_r, sr_s, sr_r, sy_s, sy_r,
    rt_s, rt_r, ty_s, ty_r,
    g0_s, g0_r, gr_s, gr_r,
    fg_s, fg_r, fs_s, fs_r,
):
    dp = lax.axis_index("dp")
    v = lax.axis_index("vocab")
    z, yh = v // 2, v % 2
    tokens, width = logits.shape
    vbase = v * width

    def at_z(k):
        other = lax.rem(z + k, NZ)
        return other, {"dp": dp, "vocab": other * 2 + yh}

    partner = {"dp": dp, "vocab": z * 2 + (1 - yh)}

    local = [
        pltpu.make_async_copy(src, dst, lsem.at[k])
        for k, (src, dst) in enumerate(
            [(pin, pinv), (hidden, hid), (labels, lab), (tgrads, tg), (pout, wv.at[pl.ds(0, RANK)])]
        )
    ]
    for copy in local:
        copy.start()
    rows_at = []
    at = 0
    for k, n in enumerate(row_chunks):
        copy = pltpu.make_async_copy(logits.at[pl.ds(at, n)], xv.at[pl.ds(at, n)], xsem.at[k])
        copy.start()
        rows_at.append((at, n, copy))
        at += n

    barrier = pltpu.get_barrier_semaphore()
    for k in range(1, NZ):
        pl.semaphore_signal(barrier, inc=1, device_id=at_z(k)[1], device_id_type=MESH)
    pl.semaphore_signal(barrier, inc=1, device_id=partner, device_id_type=MESH)

    def greet(k, c):
        pl.semaphore_signal(
            barrier, inc=1, device_id={"dp": lax.rem(dp + k, ndp), "vocab": v}, device_id_type=MESH
        )
        return c

    lax.fori_loop(1, ndp, greet, 0)

    sends = []

    def send(src, dst, ssem, rsem, device):
        copy = pltpu.make_async_remote_copy(
            src_ref=src, dst_ref=dst, send_sem=ssem, recv_sem=rsem, device_id=device, device_id_type=MESH
        )
        copy.start()
        sends.append(copy)

    def arrived(dst, sem):
        pltpu.make_async_remote_copy(
            src_ref=dst, dst_ref=dst, send_sem=sem, recv_sem=sem, device_id=partner, device_id_type=MESH
        ).wait_recv()

    local[0].wait()
    local[1].wait()
    h_part = dot_nt(pinv[...], hid[...])
    hs[:, 0:8, :] = h_part.reshape(NZ, 8, tokens)

    wv[RANK : RANK + 16, :] = jnp.ones((16, width), BF16)
    local[2].wait()
    local[4].wait()
    lab_col = jnp.transpose(jnp.broadcast_to(lab[...] - vbase, (8, tokens)).astype(F32), (1, 0))[:, 0:1]
    lab_col = lab_col.astype(jnp.int32)
    label_rows = jnp.zeros((RANK, tokens), F32)
    for lo in range(0, width, KBLOCK):
        n = min(KBLOCK, width - lo)
        hot = jnp.where(iota((tokens, n), 1) == lab_col - lo, 1.0, 0.0).astype(BF16)
        label_rows += dot_nt(wv[0:RANK, lo : lo + n], hot)
    hs[:, 8:16, :] = label_rows.reshape(NZ, 8, tokens)

    local[3].wait()
    r = iota((256, 256), 0)
    want = (r & 3) * 64 + (r >> 5) * 8 + ((r >> 2) & 1) * 4 + ((r >> 3) & 3)
    perm = jnp.where(iota((256, 256), 1) == want, 1.0, 0.0).astype(BF16)
    ts[...] = dot_nt(perm, tg[...]).astype(BF16).reshape(NZ, 32, 128)

    row = iota((16, 128), 0) >> 2
    ids = jnp.where(row == 0, gids[0], jnp.where(row == 1, gids[1], jnp.where(row == 2, gids[2], -1)))
    gs0[...] = ids.astype(F32).astype(BF16)

    parts = []
    for at, n, copy in rows_at:
        copy.wait()
        rows = pl.ds(at, n)
        whole = width // 128
        top = xv[rows, 0:128]
        for k in range(1, whole):
            top = jnp.maximum(top, xv[rows, k * 128 : (k + 1) * 128])
        top = jnp.max(top.astype(F32), axis=1, keepdims=True)
        if width % 128:
            rest = xv[rows, whole * 128 : width].astype(F32)
            top = jnp.maximum(top, jnp.max(rest, axis=1, keepdims=True))
        acc = jnp.zeros((RANK + 16, n), F32)
        for lo in range(0, width, KBLOCK):
            m = min(KBLOCK, width - lo)
            e = jnp.exp(xv[rows, lo : lo + m].astype(F32) - top).astype(BF16)
            acc += dot_nt(wv[:, lo : lo + m], e)
        ps[:, :, at : at + n] = acc[0:RANK].reshape(NZ, 8, n)
        st[1:2, at : at + n] = acc[RANK : RANK + 1]
        st[0:1, at : at + n] = jnp.transpose(jnp.broadcast_to(top, (n, 128)), (1, 0))[0:1]

    pl.semaphore_wait(barrier, NZ - 1 + 1 + ndp - 1)

    for k in range(1, NZ):
        o, device = at_z(k)
        send(hs.at[o], hr.at[z], hr_s.at[o], hr_r.at[z], device)
    for k in range(1, NZ):
        o, device = at_z(k)
        send(ps.at[o], pr.at[z], pr_s.at[o], pr_r.at[z], device)
        send(st, sr.at[z], sr_s.at[o], sr_r.at[z], device)
    for k in range(1, NZ):
        o, device = at_z(k)
        send(ts.at[o], rt.at[yh, z], rt_s.at[o], rt_r.at[z], device)
    hr[z] = hs[z]
    pr[z] = ps[z]
    sr[z] = st[...]
    rt[yh, z] = ts[z]

    def to_dp(src, dst, ssem, rsem):
        def step(k, c):
            o = lax.rem(dp + k, ndp)
            pltpu.make_async_remote_copy(
                src_ref=src, dst_ref=dst.at[dp], send_sem=ssem.at[o], recv_sem=rsem.at[dp],
                device_id={"dp": o, "vocab": v}, device_id_type=MESH,
            ).start()
            return c

        lax.fori_loop(1, ndp, step, 0)

    def from_dp(src, dst, ssem, rsem):
        def step(k, c):
            o = lax.rem(dp + k, ndp)
            pltpu.make_async_remote_copy(
                src_ref=src, dst_ref=dst.at[o], send_sem=ssem.at[o], recv_sem=rsem.at[o],
                device_id={"dp": o, "vocab": v}, device_id_type=MESH,
            ).wait_recv()
            return c

        lax.fori_loop(1, ndp, step, 0)

    def sent_dp(src, dst, ssem, rsem):
        def step(k, c):
            o = lax.rem(dp + k, ndp)
            pltpu.make_async_remote_copy(
                src_ref=src, dst_ref=dst.at[dp], send_sem=ssem.at[o], recv_sem=rsem.at[dp],
                device_id={"dp": o, "vocab": v}, device_id_type=MESH,
            ).wait_send()
            return c

        lax.fori_loop(1, ndp, step, 0)

    to_dp(gs0, gr0, g0_s, g0_r)
    gr0[dp] = gs0[...]

    for k in range(1, NZ):
        o, _ = at_z(k)
        arrived(hr.at[o], hr_r.at[o])
    total = hr[0]
    for k in range(1, NZ):
        total = total + hr[k]
    hy[yh] = total
    send(hy.at[yh], hy.at[yh], hy_s, hy_r, partner)

    for k in range(1, NZ):
        o, _ = at_z(k)
        arrived(pr.at[o], pr_r.at[o])
        arrived(sr.at[o], sr_r.at[o])

    def merged(tops, totals, products):
        peak = tops[0]
        for t in tops[1:]:
            peak = jnp.maximum(peak, t)
        total = jnp.zeros_like(peak)
        product = jnp.zeros_like(products[0])
        for t, s, p in zip(tops, totals, products):
            w = jnp.exp(t - peak)
            total = total + w * s
            product = product + w * p
        return peak, total, product

    peak, total, product = merged(
        [sr[k, 0:1] for k in range(NZ)], [sr[k, 1:2] for k in range(NZ)], [pr[k] for k in range(NZ)]
    )
    py[yh] = product
    sy[yh, 0:1] = peak
    sy[yh, 1:2] = total
    send(py.at[yh], py.at[yh], py_s, py_r, partner)
    send(sy.at[yh], sy.at[yh], sy_s, sy_r, partner)

    arrived(hy.at[1 - yh], hy_r)
    both = hy[0] + hy[1]
    label_part = both[8:16]
    hb[...] = both[0:8].astype(BF16)
    for k in range(1, NZ):
        o, device = at_z(k)
        send(hb, hall.at[z], hb_s.at[o], hb_r.at[z], device)
    hall[z] = hb[...]

    arrived(py.at[1 - yh], py_r)
    arrived(sy.at[1 - yh], sy_r)
    peak, total, product = merged(
        [sy[k, 0:1] for k in range(2)], [sy[k, 1:2] for k in range(2)], [py[k] for k in range(2)]
    )
    rproj = product / total - label_part

    for k in range(1, NZ):
        o, _ = at_z(k)
        arrived(rt.at[yh, o], rt_r.at[o])
    send(rt.at[yh], rt.at[yh], ty_s, ty_r, partner)

    spans = tokens // SPAN
    span_of = iota((8, tokens), 1) // SPAN
    high = rproj.astype(BF16)
    low = (rproj - high.astype(F32)).astype(BF16)
    zero = jnp.zeros_like(rproj)
    lhs = []
    for s in range(spans):
        lhs.append(jnp.where(span_of == s, high.astype(F32), zero))
        lhs.append(jnp.where(span_of == s, low.astype(F32), zero))
    lhs = jnp.concatenate(lhs, 0).astype(BF16)

    for k in range(1, NZ):
        o, _ = at_z(k)
        arrived(hall.at[o], hb_r.at[o])
    hproj = hall[...].reshape(RANK, tokens)
    outer = dot_nt(lhs, jnp.concatenate([hproj, hproj], 0))
    lane = iota((8, 128), 1)
    low_rows = iota((8, 128), 0) < 4
    tiles = []
    for s in range(spans):
        a = outer[16 * s : 16 * s + 8] + outer[16 * s + 8 : 16 * s + 16]
        tiles.append(jnp.where(lane < 64, a, pltpu.roll(a, 4, 0)))
    first = jnp.where(low_rows, tiles[0], pltpu.roll(tiles[1], 4, 0))
    second = jnp.where(low_rows, tiles[2], 0.0)
    gs[...] = jnp.concatenate([first, second], 0).astype(BF16)
    to_dp(gs, gr, gr_s, gr_r)
    gr[dp] = gs[...]

    from_dp(gs0, gr0, g0_s, g0_r)
    nrows = ndp * 16
    gid = gr0[...].reshape(nrows, 128).astype(F32)
    member = jnp.where(gid == iota((nrows, 128), 1).astype(F32), 1.0, 0.0)
    member = jnp.transpose(member, (1, 0))[0:GROUPS]
    rr, col = iota((64, nrows), 0), iota((64, nrows), 1)
    a, zz = rr & 7, rr >> 3
    late = (a >= 3).astype(jnp.int32)
    source = 4 * (2 * (2 * zz + yh) + late) + (a - 3 * late)
    pick = jnp.where(((col >> 2) == source) & (a < 6), 1.0, 0.0)
    cmat[...] = jnp.concatenate([member, pick], 0).astype(BF16)

    arrived(rt.at[1 - yh], ty_r)
    tests = rt[...].reshape(512, 128)
    for jp in range(4):
        r = iota((128, 512), 0)
        i = r & 63
        want = ((i >> 2) & 1) * 256 + (i >> 3) * 32 + jp * 8 + (r >> 6) * 4 + (i & 3)
        perm = jnp.where(iota((128, 512), 1) == want, 1.0, 0.0).astype(BF16)
        tb[jp] = dot(perm, tests).astype(BF16)

    from_dp(gs, gr, gr_s, gr_r)
    grads = gr[...].reshape(nrows, 128)
    jrow = iota((nrows, 128), 0) & 3
    value = dot(grads, tb[0])
    for jp in range(1, 4):
        value = jnp.where(jrow == jp, dot(grads, tb[jp]), value)
    one = value.astype(BF16)
    rest = value - one.astype(F32)
    two = rest.astype(BF16)
    three = (rest - two.astype(F32)).astype(BF16)
    c = cmat[...]
    summed = (dot(c, three) + dot(c, two)) + dot(c, one)
    fg[...] = summed[0:GROUPS]
    fs[...] = summed[GROUPS:].reshape(NZ, 8, 128)
    for k in range(1, NZ):
        o, device = at_z(k)
        send(fs.at[o], fsr.at[z], fs_s.at[o], fs_r.at[z], device)
        send(fg, fgr.at[z], fg_s.at[o], fg_r.at[z], device)
    fsr[z] = fs[z]
    fgr[z] = fg[...]
    for k in range(1, NZ):
        o, _ = at_z(k)
        arrived(fsr.at[o], fs_r.at[o])
        arrived(fgr.at[o], fg_r.at[o])
    a, b = fsr[0], fgr[0]
    for k in range(1, NZ):
        a, b = a + fsr[k], b + fgr[k]
    out_s[...] = a[0:6]
    out_g[...] = b

    for copy in sends:
        copy.wait_send()
    sent_dp(gs0, gr0, g0_s, g0_r)
    sent_dp(gs, gr, gr_s, gr_r)


def per_device(ndp, logits, labels, hidden, proj_in, proj_out, test_grads, group_ids):
    tokens, width = logits.shape
    any_spec = pl.BlockSpec(memory_space=pl.ANY)
    vmem = pl.BlockSpec(memory_space=pltpu.VMEM)
    dma, V = pltpu.SemaphoreType.DMA, pltpu.VMEM
    row_chunks = (64, 128)
    return pl.pallas_call(
        functools.partial(kernel, ndp, row_chunks),
        name="scores",
        out_shape=(
            jax.ShapeDtypeStruct((6, 128), F32),
            jax.ShapeDtypeStruct((GROUPS, 128), F32),
        ),
        in_specs=[any_spec] * 6 + [pl.BlockSpec(memory_space=pltpu.SMEM)],
        out_specs=(vmem, vmem),
        scratch_shapes=[
            V((tokens, width), BF16), V((RANK + 16, width), BF16), V((1, tokens), jnp.int32),
            V((tokens, 256), BF16), V((RANK, 256), BF16), V((128, 256), BF16),
            V((NZ, 16, tokens), F32), V((NZ, 16, tokens), F32), V((2, 16, tokens), F32),
            V((8, tokens), BF16), V((NZ, 8, tokens), BF16),
            V((NZ, 8, tokens), F32), V((NZ, 8, tokens), F32), V((2, 8, tokens), F32),
            V((2, tokens), F32), V((NZ, 2, tokens), F32), V((2, 2, tokens), F32),
            V((NZ, 32, 128), BF16), V((2, NZ, 32, 128), BF16), V((4, 128, 128), BF16),
            V((16, 128), BF16), V((ndp, 16, 128), BF16), V((16, 128), BF16), V((ndp, 16, 128), BF16),
            V((96, ndp * 16), BF16),
            V((GROUPS, 128), F32), V((NZ, GROUPS, 128), F32), V((NZ, 8, 128), F32), V((NZ, 8, 128), F32),
            dma((5,)), dma((len(row_chunks),)),
            dma((NZ,)), dma((NZ,)), dma, dma, dma((NZ,)), dma((NZ,)),
            dma((NZ,)), dma((NZ,)), dma, dma, dma((NZ,)), dma((NZ,)), dma, dma,
            dma((NZ,)), dma((NZ,)), dma, dma,
            dma((ndp,)), dma((ndp,)), dma((ndp,)), dma((ndp,)),
            dma((NZ,)), dma((NZ,)), dma((NZ,)), dma((NZ,)),
        ],
        compiler_params=pltpu.CompilerParams(collective_id=0, has_side_effects=True),
    )(logits, labels.reshape(1, tokens), hidden, proj_in.T, proj_out.T, test_grads, group_ids)


def solution(mesh):
    in_specs = (
        P("dp", "vocab"),
        P("dp"),
        P("dp", "vocab"),
        P("vocab", None),
        P("vocab", None),
        P("dp", "vocab"),
        P("dp"),
    )
    out_specs = (P("vocab", "dp"), P(None, "dp"))
    return jax.shard_map(
        functools.partial(per_device, mesh.shape["dp"]),
        mesh=mesh, in_specs=in_specs, out_specs=out_specs, check_vma=False,
    )
```

```python
import functools

import jax
import jax.numpy as jnp
from jax import lax
from jax.experimental import pallas as pl
from jax.experimental.pallas import tpu as pltpu
from jax.sharding import PartitionSpec as P

RANK = 64
SPAN = 64
GROUPS = 32
MESH = pl.DeviceIdType.MESH
F32 = jnp.float32
BF16 = jnp.bfloat16
NT = (((1,), (1,)), ((), ()))
NZ = 8
KBLOCK = 1024


def dot(a, b):
    return jnp.dot(a, b, preferred_element_type=F32)


def dot_nt(a, b):
    return lax.dot_general(a, b, NT, preferred_element_type=F32)


def iota(shape, dim):
    return lax.broadcasted_iota(jnp.int32, shape, dim)


def kernel(
    ndp, row_chunks,
    logits, labels, hidden, pin, pout, tgrads, gids,
    out_s, out_g,
    xv, wv, lab, gid, hid, pinv, tg,
    hp, hy, hz, hr,
    ps, pr, py, st, sr, sy,
    ls, lr, ly,
    ts, rt, tb,
    gs0, gr0, gs, gr, cmat,
    fg, fgr, fs, fsr,
    lsem, xsem,
    hy_s, hy_r, hz_s, hz_r,
    pr_s, pr_r, py_s, py_r, sr_s, sr_r, sy_s, sy_r,
    lr_s, lr_r, ly_s, ly_r,
    rt_s, rt_r, ty_s, ty_r,
    g0_s, g0_r, gr_s, gr_r,
    fg_s, fg_r, fs_s, fs_r,
):
    dp = lax.axis_index("dp")
    v = lax.axis_index("vocab")
    z, yh = v // 2, v % 2
    tokens, width = logits.shape
    spans = tokens // SPAN
    vbase = v * width

    def at_z(k):
        other = lax.rem(z + k, NZ)
        return other, {"dp": dp, "vocab": other * 2 + yh}

    partner = {"dp": dp, "vocab": z * 2 + (1 - yh)}

    local = [
        pltpu.make_async_copy(src, dst, lsem.at[k])
        for k, (src, dst) in enumerate(
            [(pin, pinv), (hidden, hid), (pout, wv.at[pl.ds(0, RANK)]), (labels, lab), (tgrads, tg), (gids, gid)]
        )
    ]
    for copy in local[:3]:
        copy.start()
    rows_at = []
    at = 0
    for k, n in enumerate(row_chunks):
        copy = pltpu.make_async_copy(logits.at[pl.ds(at, n)], xv.at[pl.ds(at, n)], xsem.at[k])
        copy.start()
        rows_at.append((at, n, copy))
        at += n
    for copy in local[3:]:
        copy.start()

    barrier = pltpu.get_barrier_semaphore()

    other_row = [lax.rem(dp + ndp // 2 + k, ndp) for k in range(ndp) if k != ndp // 2]
    plane = [{"dp": o, "vocab": z * 2 + (1 - yh)} for o in other_row]
    plane += [{"dp": o, "vocab": v} for o in other_row] + [partner]

    for device in plane:
        pl.semaphore_signal(barrier, inc=1, device_id=device, device_id_type=MESH)
    for k in range(1, NZ):
        pl.semaphore_signal(barrier, inc=1, device_id=at_z(k)[1], device_id_type=MESH)

    sends = []

    def send(src, dst, ssem, rsem, device):
        pltpu.make_async_remote_copy(
            src_ref=src, dst_ref=dst, send_sem=ssem, recv_sem=rsem, device_id=device, device_id_type=MESH
        ).start()

    def arrived(ref, sem):
        pltpu.make_async_remote_copy(
            src_ref=ref, dst_ref=ref, send_sem=sem, recv_sem=sem, device_id=partner, device_id_type=MESH
        ).wait_recv()

    def sent(ref, sem):
        sends.append((ref, sem))

    def drain():
        for ref, sem in sends:
            pltpu.make_async_remote_copy(
                src_ref=ref, dst_ref=ref, send_sem=sem, recv_sem=sem, device_id=partner, device_id_type=MESH
            ).wait_send()
        sends.clear()

    def seven(ref):
        return ref.at[pl.ds(0, NZ - 1)]

    wv[RANK : RANK + 16, :] = jnp.ones((16, width), BF16)
    local[0].wait()
    local[1].wait()
    r = iota((RANK, RANK), 0)
    want = ((r >> 2) & 7) * 8 + (r >> 5) * 4 + (r & 3)
    perm = jnp.where(iota((RANK, RANK), 1) == want, 1.0, 0.0).astype(BF16)
    pin_rows = dot(perm, pinv[...]).astype(BF16)
    hp[...] = dot_nt(pin_rows, hid[...]).reshape(2, 32, tokens)

    local[2].wait()
    for at, n, copy in rows_at:
        copy.wait()
        rows = pl.ds(at, n)
        whole = width // 128
        top = xv[rows, 0:128]
        for k in range(1, whole):
            top = jnp.maximum(top, xv[rows, k * 128 : (k + 1) * 128])
        top = jnp.max(top.astype(F32), axis=1, keepdims=True)
        if width % 128:
            rest = xv[rows, whole * 128 : width].astype(F32)
            top = jnp.maximum(top, jnp.max(rest, axis=1, keepdims=True))
        acc = jnp.zeros((RANK + 16, n), F32)
        for lo in range(0, width, KBLOCK):
            m = min(KBLOCK, width - lo)
            e = jnp.exp(xv[rows, lo : lo + m].astype(F32) - top).astype(BF16)
            acc += dot_nt(wv[:, lo : lo + m], e)
        ps[:, :, at : at + n] = acc[0:RANK].reshape(NZ, 8, n)
        st[1:2, at : at + n] = acc[RANK : RANK + 1]
        st[0:1, at : at + n] = jnp.transpose(jnp.broadcast_to(top, (n, 128)), (1, 0))[0:1]

    pl.semaphore_wait(barrier, NZ - 1 + 2 * ndp - 1)

    send(hp.at[1 - yh], hy, hy_s, hy_r, partner)
    for k in range(1, NZ):
        o, device = at_z(k)
        send(ps.at[o], pr.at[z], pr_s, pr_r, device)
        send(st, sr.at[z], sr_s, sr_r, device)
    pr[z] = ps[z]
    sr[z] = st[...]

    local[3].wait()
    label_rows = jnp.zeros((RANK, tokens), F32)
    lab_row = lab[...] - vbase
    for lo in range(0, width, KBLOCK):
        n = min(KBLOCK, width - lo)
        hot = jnp.where(iota((n, tokens), 0) == lab_row - lo, 1.0, 0.0).astype(BF16)
        label_rows += dot(wv[0:RANK, lo : lo + n], hot)
    ls[...] = label_rows.reshape(NZ, 8, tokens).astype(BF16)
    for k in range(1, NZ):
        o, device = at_z(k)
        send(ls.at[o], lr.at[z], lr_s, lr_r, device)
    lr[z] = ls[z]

    local[4].wait()
    r = iota((256, 256), 0)
    want = (r & 3) * 64 + (r >> 5) * 8 + ((r >> 2) & 3) * 2 + ((r >> 4) & 1)
    perm = jnp.where(iota((256, 256), 1) == want, 1.0, 0.0).astype(BF16)
    ts[...] = dot_nt(perm, tg[...]).astype(BF16).reshape(NZ, 32, 128)
    local[5].wait()
    srow = iota((8, 128), 0) >> 1
    ids = jnp.full((8, 128), -1, jnp.int32)
    for s in range(spans):
        ids = jnp.where(srow == s, jnp.broadcast_to(gid[0:1, s : s + 1], (8, 128)), ids)
    gs0[...] = ids.astype(F32).astype(BF16)

    for k in range(1, NZ):
        o, device = at_z(k)
        send(ts.at[o], rt.at[yh, z], rt_s, rt_r, device)
    rt[yh, z] = ts[z]

    for o in other_row:
        send(gs0, gr0.at[dp], g0_s, g0_r, {"dp": o, "vocab": v})
    gr0[dp] = gs0[...]

    arrived(hy, hy_r)
    hz[...] = (hp[yh] + hy[...]).astype(BF16)
    for k in range(1, NZ):
        o, device = at_z(k)
        send(hz, hr.at[z], hz_s, hz_r, device)
    hr[z] = hz[...]

    def merged(tops, totals, products):
        peak = tops[0]
        for t in tops[1:]:
            peak = jnp.maximum(peak, t)
        total = jnp.zeros_like(peak)
        product = jnp.zeros_like(products[0])
        for t, s, p in zip(tops, totals, products):
            w = jnp.exp(t - peak)
            total = total + w * s
            product = product + w * p
        return peak, total, product

    arrived(seven(pr), pr_r)
    arrived(seven(sr), sr_r)
    peak, total, product = merged(
        [sr[k, 0:1] for k in range(NZ)], [sr[k, 1:2] for k in range(NZ)], [pr[k] for k in range(NZ)]
    )
    py[yh] = product
    sy[yh, 0:1] = peak
    sy[yh, 1:2] = total
    send(py.at[yh], py.at[yh], py_s, py_r, partner)
    send(sy.at[yh], sy.at[yh], sy_s, sy_r, partner)

    arrived(seven(lr), lr_r)
    label_part = lr[0].astype(F32)
    for k in range(1, NZ):
        label_part = label_part + lr[k].astype(F32)
    ly[yh] = label_part.astype(BF16)
    send(ly.at[yh], ly.at[yh], ly_s, ly_r, partner)

    arrived(seven(rt.at[yh]), rt_r)
    send(rt.at[yh], rt.at[yh], ty_s, ty_r, partner)

    arrived(seven(hr), hz_r)
    hproj = hr[0].astype(F32)
    for k in range(1, NZ):
        hproj = hproj + hr[k].astype(F32)
    h_high = hproj.astype(BF16)
    h_low = (hproj - h_high.astype(F32)).astype(BF16)
    rhs = jnp.concatenate([h_high] * 4 + [h_low] * 4, 0)

    arrived(py.at[1 - yh], py_r)
    arrived(sy.at[1 - yh], sy_r)
    arrived(ly.at[1 - yh], ly_r)
    peak, total, product = merged(
        [sy[k, 0:1] for k in range(2)], [sy[k, 1:2] for k in range(2)], [py[k] for k in range(2)]
    )
    rproj = product / total - (ly[0].astype(F32) + ly[1].astype(F32))

    span_of = iota((8, tokens), 1) // SPAN
    high = rproj.astype(BF16).astype(F32)
    low = rproj - high
    lhs = [jnp.where(span_of == s, high, 0.0) for s in range(spans)]
    lhs += [jnp.where(span_of == s, low, 0.0) for s in range(spans)]
    outer = dot_nt(jnp.concatenate(lhs, 0).astype(BF16), rhs)
    outer = (outer[0 : 8 * spans, 128:] + outer[8 * spans :, 0:128]) + outer[0 : 8 * spans, 0:128]
    block = iota((8, 128), 1) // 32
    pair = iota((8, 128), 0) >> 1
    tile = jnp.zeros((8, 128), F32)
    for s in range(spans):
        a = outer[8 * s : 8 * s + 8]
        for jq in range(4):
            shift = (2 * s - 2 * jq) % 8
            moved = pltpu.roll(a, shift, 0) if shift else a
            tile = jnp.where((pair == s) & (block == jq), moved, tile)
    gs[...] = tile.astype(BF16)

    me = yh * ndp + dp

    for device in plane:
        send(gs, gr.at[me], gr_s, gr_r, device)
    gr[me] = gs[...]

    arrived(gr0.at[pl.ds(0, ndp - 1)], g0_r)
    nrows = ndp * 8
    groups = gr0[...].reshape(nrows, 128).astype(F32)
    member = jnp.where(groups == iota((nrows, 128), 1).astype(F32), 1.0, 0.0)
    member = jnp.transpose(member, (1, 0))[0:GROUPS]
    rr, col = iota((64, nrows), 0), iota((64, nrows), 1)
    a, zz = rr & 7, rr >> 3
    late = (a >= 3).astype(jnp.int32)
    source = 4 * (2 * (2 * zz + yh) + late) + (a - 3 * late)
    pick = jnp.where(((col >> 1) == source) & (a < 6), 1.0, 0.0)
    cmat[...] = jnp.concatenate([member, pick], 0).astype(BF16)

    sent(hy, hy_s)
    sent(seven(hr), hz_s)
    sent(seven(pr), pr_s)
    sent(seven(sr), sr_s)
    sent(seven(lr), lr_s)
    sent(seven(rt.at[yh]), rt_s)
    sent(py.at[0], py_s)
    sent(sy.at[0], sy_s)
    sent(ly.at[0], ly_s)
    sent(rt.at[0], ty_s)
    sent(gr0.at[pl.ds(0, ndp - 1)], g0_s)
    drain()

    arrived(rt.at[1 - yh], ty_r)
    r = iota((256, 256), 0)
    want = ((r >> 2) & 7) * 32 + (r >> 7) * 16 + ((r >> 5) & 3) * 4 + (r & 3)
    perm = jnp.where(iota((256, 256), 1) == want, 1.0, 0.0).astype(BF16)
    for y in range(2):
        tb[y] = dot(perm, rt[y].reshape(256, 128)).astype(BF16).reshape(2, 128, 128)

    arrived(gr.at[pl.ds(0, 2 * ndp - 1)], gr_r)

    jrow = iota((nrows, 128), 0) & 1
    value = jnp.zeros((nrows, 128), F32)
    for y in range(2):
        grads = gr[pl.ds(y * ndp, ndp)].reshape(nrows, 128)
        value += jnp.where(jrow == 0, dot(grads, tb[y, 0]), dot(grads, tb[y, 1]))
    one = value.astype(BF16)
    rest = value - one.astype(F32)
    two = rest.astype(BF16)
    three = (rest - two.astype(F32)).astype(BF16)
    c = cmat[...]
    summed = (dot(c, three) + dot(c, two)) + dot(c, one)
    fg[...] = summed[0:GROUPS]
    fs[...] = summed[GROUPS:].reshape(NZ, 8, 128)

    for k in range(1, NZ):
        o, device = at_z(k)
        send(fs.at[o], fsr.at[z], fs_s, fs_r, device)
        send(fg, fgr.at[z], fg_s, fg_r, device)
    fsr[z] = fs[z]
    fgr[z] = fg[...]

    sent(gr.at[pl.ds(0, 2 * ndp - 1)], gr_s)
    sent(seven(fsr), fs_s)
    sent(seven(fgr), fg_s)
    drain()

    arrived(seven(fsr), fs_r)
    arrived(seven(fgr), fg_r)

    for half in range(2):
        a, b = fsr[4 * half], fgr[4 * half]
        for k in range(4 * half + 1, 4 * half + 4):
            a, b = a + fsr[k], b + fgr[k]
        out_s[half] = a
        out_g[half] = b


def per_device(ndp, logits, labels, hidden, proj_in, proj_out, test_grads, group_ids):
    tokens, width = logits.shape
    any_spec = pl.BlockSpec(memory_space=pl.ANY)
    vmem = pl.BlockSpec(memory_space=pltpu.VMEM)
    dma, V = pltpu.SemaphoreType.DMA, pltpu.VMEM
    row_chunks = (64, 64, 64)
    s, g = pl.pallas_call(
        functools.partial(kernel, ndp, row_chunks),
        name="scores",
        out_shape=(
            pltpu.VMEM((2, 8, 128), F32),
            pltpu.VMEM((2, GROUPS, 128), F32),
        ),
        in_specs=[any_spec] * 7,
        out_specs=(vmem, vmem),
        scratch_shapes=[
            V((tokens, width), BF16), V((RANK + 16, width), BF16), V((1, tokens), jnp.int32), V((1, 3), jnp.int32),
            V((tokens, 256), BF16), V((RANK, 256), BF16), V((128, 256), BF16),
            V((2, 32, tokens), F32), V((32, tokens), F32), V((32, tokens), BF16), V((NZ, 32, tokens), BF16),
            V((NZ, 8, tokens), F32), V((NZ, 8, tokens), F32), V((2, 8, tokens), F32),
            V((2, tokens), F32), V((NZ, 2, tokens), F32), V((2, 2, tokens), F32),
            V((NZ, 8, tokens), BF16), V((NZ, 8, tokens), BF16), V((2, 8, tokens), BF16),
            V((NZ, 32, 128), BF16), V((2, NZ, 32, 128), BF16), V((2, 2, 128, 128), BF16),
            V((8, 128), BF16), V((ndp, 8, 128), BF16), V((8, 128), BF16), V((2 * ndp, 8, 128), BF16),
            V((96, ndp * 8), BF16),
            V((GROUPS, 128), F32), V((NZ, GROUPS, 128), F32), V((NZ, 8, 128), F32), V((NZ, 8, 128), F32),
            dma((6,)), dma((len(row_chunks),)),
            *[dma] * 28,
        ],
        compiler_params=pltpu.CompilerParams(collective_id=0, has_side_effects=True),
    )(
        logits, labels.reshape(1, tokens), hidden, proj_in.T, proj_out.T, test_grads,
        group_ids.reshape(1, 3),
    )
    return jnp.sum(s, axis=0)[0:6], jnp.sum(g, axis=0)


def solution(mesh):
    in_specs = (
        P("dp", "vocab"),
        P("dp"),
        P("dp", "vocab"),
        P("vocab", None),
        P("vocab", None),
        P("dp", "vocab"),
        P("dp"),
    )
    out_specs = (P("vocab", "dp"), P(None, "dp"))
    return jax.shard_map(
        functools.partial(per_device, mesh.shape["dp"]),
        mesh=mesh, in_specs=in_specs, out_specs=out_specs, check_vma=False,
    )
```

```python
import functools

import jax
import jax.numpy as jnp
from jax import lax
from jax.experimental import pallas as pl
from jax.experimental.pallas import tpu as pltpu
from jax.sharding import PartitionSpec as P

RANK = 64
SPAN = 64
GROUPS = 32
MESH = pl.DeviceIdType.MESH
F32 = jnp.float32
BF16 = jnp.bfloat16
NT = (((1,), (1,)), ((), ()))
NZ = 8
KBLOCK = 1024
EARLY = 5


def dot(a, b):
    return jnp.dot(a, b, preferred_element_type=F32)


def dot_nt(a, b):
    return lax.dot_general(a, b, NT, preferred_element_type=F32)


def iota(shape, dim):
    return lax.broadcasted_iota(jnp.int32, shape, dim)


def kernel(
    ndp, row_chunks,
    logits, labels, hidden, pin, pout, tgrads, gids,
    out_s, out_g,
    xv, wv, lab, gid, hid, pinv, tg,
    hp, hb, hy, hz, hr,
    ps, pr, py, st, sr, sy,
    ls, lr, ly,
    ts, rt, tb,
    gs0, gr0, gs, gr, cmat, vals,
    fg, fgr, fs, fsr,
    lsem, xsem,
    hy_s, hy_r, hz_s, hz_r,
    pr_s, pr_r, py_s, py_r, sr_s, sr_r, sy_s, sy_r,
    lr_s, lr_r, ly_s, ly_r,
    rt_s, rt_r, ty_s, ty_r,
    g0_s, g0_r, i_s, i_r, gr_s, grn_r, grf_r, fn_s, fn_r, ff_s, ff_r,
    fg_s, fg_r, fs_s, fs_r,
):
    dp = lax.axis_index("dp")
    v = lax.axis_index("vocab")
    z, yh = v // 2, v % 2
    tokens, width = logits.shape
    spans = tokens // SPAN
    vbase = v * width

    def at_z(k):
        other = lax.rem(z + k, NZ)
        return other, {"dp": dp, "vocab": other * 2 + yh}

    partner = {"dp": dp, "vocab": z * 2 + (1 - yh)}

    local = [
        pltpu.make_async_copy(src, dst, lsem.at[k])
        for k, (src, dst) in enumerate(
            [(pin, pinv), (hidden, hid), (tgrads, tg), (pout, wv.at[pl.ds(0, RANK)]), (labels, lab), (gids, gid)]
        )
    ]
    for copy in local[:3]:
        copy.start()
    rows_at = []
    at = 0
    for k, n in enumerate(row_chunks):
        copy = pltpu.make_async_copy(logits.at[pl.ds(at, n)], xv.at[pl.ds(at, n)], xsem.at[k])
        copy.start()
        if k == 0:
            local[3].start()
        rows_at.append((at, n, copy))
        at += n
    for copy in local[4:]:
        copy.start()

    barrier = pltpu.get_barrier_semaphore()

    core, place = lax.rem(dp, 2), dp // 2
    nplace = ndp // 2
    places = [lax.rem(place + nplace // 2 + k, nplace) for k in range(nplace) if k != nplace // 2]
    far = [{"dp": 2 * o + core, "vocab": z * 2 + (1 - yh)} for o in places] + [partner]
    near = [{"dp": 2 * o + core, "vocab": v} for o in places]
    sibling = {"dp": dp + 1 - 2 * core, "vocab": v}

    for device in far + near + [sibling]:
        pl.semaphore_signal(barrier, inc=1, device_id=device, device_id_type=MESH)
    for k in range(1, NZ):
        pl.semaphore_signal(barrier, inc=1, device_id=at_z(k)[1], device_id_type=MESH)

    sends = []

    def send(src, dst, ssem, rsem, device):
        pltpu.make_async_remote_copy(
            src_ref=src, dst_ref=dst, send_sem=ssem, recv_sem=rsem, device_id=device, device_id_type=MESH
        ).start()

    def arrived(ref, sem):
        pltpu.make_async_remote_copy(
            src_ref=ref, dst_ref=ref, send_sem=sem, recv_sem=sem, device_id=partner, device_id_type=MESH
        ).wait_recv()

    def sent(ref, sem):
        sends.append((ref, sem))

    def drain():
        for ref, sem in sends:
            pltpu.make_async_remote_copy(
                src_ref=ref, dst_ref=ref, send_sem=sem, recv_sem=sem, device_id=partner, device_id_type=MESH
            ).wait_send()
        sends.clear()

    def seven(ref):
        return ref.at[pl.ds(0, NZ - 1)]

    wv[RANK : RANK + 16, :] = jnp.ones((16, width), BF16)
    local[0].wait()
    local[1].wait()
    r = iota((RANK, RANK), 0)
    want = ((r >> 2) & 7) * 8 + (r >> 5) * 4 + (r & 3)
    perm = jnp.where(iota((RANK, RANK), 1) == want, 1.0, 0.0).astype(BF16)
    pin_rows = dot(perm, pinv[...]).astype(BF16)
    h_part = dot_nt(pin_rows, hid[...])
    for y in range(2):
        side = h_part[32 * y : 32 * y + 32]
        hp[y, 0:32] = side[:, 0:128]
        hp[y, 32:48] = jnp.concatenate([side[0:16, 128:], side[16:, 128:]], 1)
    hb[...] = hp[...].astype(BF16)

    local[2].wait()
    r = iota((256, 256), 0)
    want = (r & 3) * 64 + (r >> 5) * 8 + ((r >> 2) & 3) * 2 + ((r >> 4) & 1)
    perm = jnp.where(iota((256, 256), 1) == want, 1.0, 0.0).astype(BF16)
    ts[...] = dot_nt(perm, tg[...]).astype(BF16).reshape(NZ, 32, 128)
    whole = width // 128

    def top_of(at, n):
        rows = pl.ds(at, n)
        top = xv[rows, 0:128]
        for k in range(1, whole):
            top = jnp.maximum(top, xv[rows, k * 128 : (k + 1) * 128])
        top = jnp.max(top.astype(F32), axis=1, keepdims=True)
        if width % 128:
            rest = xv[rows, whole * 128 : width].astype(F32)
            top = jnp.maximum(top, jnp.max(rest, axis=1, keepdims=True))
        return top

    def product_of(at, n, top, los):
        acc = jnp.zeros((RANK + 16, n), F32)
        for lo in los:
            m = min(KBLOCK, width - lo)
            e = jnp.exp(xv[pl.ds(at, n), lo : lo + m].astype(F32) - top).astype(BF16)
            acc += dot_nt(wv[:, lo : lo + m], e)
        return acc

    def keep(at, n, top, acc):
        ps[:, :, at : at + n] = acc[0:RANK].reshape(NZ, 8, n)
        st[1:2, at : at + n] = acc[RANK : RANK + 1]
        st[0:1, at : at + n] = jnp.transpose(jnp.broadcast_to(top, (n, 128)), (1, 0))[0:1]

    los = list(range(0, width, KBLOCK))
    (at, n, copy), (at2, n2, copy2) = rows_at
    copy.wait()
    top = top_of(at, n)
    local[3].wait()
    acc = product_of(at, n, top, los[:EARLY])
    copy2.wait()
    acc += product_of(at, n, top, los[EARLY:])
    top2 = top_of(at2, n2)
    keep(at, n, top, acc)
    keep(at2, n2, top2, product_of(at2, n2, top2, los))

    pl.semaphore_wait(barrier, NZ - 1 + ndp)

    send(hb.at[1 - yh], hy, hy_s, hy_r, partner)
    for k in range(1, NZ):
        o, device = at_z(k)
        send(ps.at[o], pr.at[z], pr_s, pr_r, device)
        send(st, sr.at[z], sr_s, sr_r, device)
    pr[z] = ps[z]
    sr[z] = st[...]

    local[4].wait()
    label_rows = jnp.zeros((RANK, tokens), F32)
    lab_row = lab[...] - vbase
    hot = jnp.where(iota((256, tokens), 0) == (lab_row & 255), 1.0, 0.0).astype(BF16)
    lab_block = lab_row >> 8
    for lo in range(0, width, 256):
        n = min(256, width - lo)
        label_rows = jnp.where(lab_block == lo >> 8, dot(wv[0:RANK, lo : lo + n], hot[0:n]), label_rows)
    ls[...] = label_rows.reshape(NZ, 8, tokens).astype(BF16)
    for k in range(1, NZ):
        o, device = at_z(k)
        send(ls.at[o], lr.at[z], lr_s, lr_r, device)
    for k in range(1, NZ):
        o, device = at_z(k)
        send(ts.at[o], rt.at[yh, z], rt_s, rt_r, device)
    lr[z] = ls[z]
    rt[yh, z] = ts[z]

    local[5].wait()
    srow = iota((8, 128), 0) >> 1
    ids = jnp.full((8, 128), -1, jnp.int32)
    for s in range(spans):
        ids = jnp.where(srow == s, jnp.broadcast_to(gid[0:1, s : s + 1], (8, 128)), ids)
    gs0[...] = ids.astype(F32).astype(BF16)

    for o in places:
        send(gs0, gr0.at[core * nplace + place], g0_s, g0_r, {"dp": 2 * o + core, "vocab": v})
    gr0[core * nplace + place] = gs0[...]

    arrived(hy, hy_r)
    hz[...] = (hp[yh] + hy[...].astype(F32)).astype(BF16)
    for k in range(1, NZ):
        o, device = at_z(k)
        send(hz, hr.at[z], hz_s, hz_r, device)
    hr[z] = hz[...]

    def merged(tops, totals, products):
        peak = tops[0]
        for t in tops[1:]:
            peak = jnp.maximum(peak, t)
        total = jnp.zeros_like(peak)
        product = jnp.zeros_like(products[0])
        for t, s, p in zip(tops, totals, products):
            w = jnp.exp(t - peak)
            total = total + w * s
            product = product + w * p
        return peak, total, product

    arrived(seven(pr), pr_r)
    arrived(seven(sr), sr_r)
    peak, total, product = merged(
        [sr[k, 0:1] for k in range(NZ)], [sr[k, 1:2] for k in range(NZ)], [pr[k] for k in range(NZ)]
    )
    py[yh] = product
    sy[yh, 0:1] = peak
    sy[yh, 1:2] = total
    send(py.at[yh], py.at[yh], py_s, py_r, partner)
    send(sy.at[yh], sy.at[yh], sy_s, sy_r, partner)

    arrived(seven(lr), lr_r)
    label_part = lr[0].astype(F32)
    for k in range(1, NZ):
        label_part = label_part + lr[k].astype(F32)
    ly[yh] = label_part.astype(BF16)
    send(ly.at[yh], ly.at[yh], ly_s, ly_r, partner)

    arrived(seven(rt.at[yh]), rt_r)
    send(rt.at[yh], rt.at[yh], ty_s, ty_r, partner)

    arrived(seven(hr), hz_r)
    packed = hr[0].astype(F32)
    for k in range(1, NZ):
        packed = packed + hr[k].astype(F32)
    hproj = jnp.concatenate(
        [packed[0:32], jnp.concatenate([packed[32:48, 0:64], packed[32:48, 64:]], 0)], 1
    )
    h_high = hproj.astype(BF16)
    h_low = (hproj - h_high.astype(F32)).astype(BF16)
    rhs = jnp.concatenate([h_high] * 4 + [h_low] * 4, 0)

    arrived(py.at[1 - yh], py_r)
    arrived(sy.at[1 - yh], sy_r)
    arrived(ly.at[1 - yh], ly_r)
    peak, total, product = merged(
        [sy[k, 0:1] for k in range(2)], [sy[k, 1:2] for k in range(2)], [py[k] for k in range(2)]
    )
    rproj = product / total - (ly[0].astype(F32) + ly[1].astype(F32))

    span_of = iota((8, tokens), 1) // SPAN
    high = rproj.astype(BF16).astype(F32)
    low = rproj - high
    lhs = [jnp.where(span_of == s, high, 0.0) for s in range(spans)]
    lhs += [jnp.where(span_of == s, low, 0.0) for s in range(spans)]
    outer = dot_nt(jnp.concatenate(lhs, 0).astype(BF16), rhs)
    outer = (outer[0 : 8 * spans, 128:] + outer[8 * spans :, 0:128]) + outer[0 : 8 * spans, 0:128]
    block = iota((8, 128), 1) // 32
    pair = iota((8, 128), 0) >> 1
    tile = jnp.zeros((8, 128), F32)
    for s in range(spans):
        a = outer[8 * s : 8 * s + 8]
        for jq in range(4):
            shift = (2 * s - 2 * jq) % 8
            moved = pltpu.roll(a, shift, 0) if shift else a
            tile = jnp.where((pair == s) & (block == jq), moved, tile)
    gs[...] = tile.astype(BF16)

    half = 2 * nplace
    me = core * half + yh * nplace + place
    for device in far:
        send(gs, gr.at[me], gr_s, grf_r, device)
    for device in near:
        send(gs, gr.at[me], gr_s, grn_r, device)
    gr[me] = gs[...]

    arrived(gr0.at[pl.ds(0, nplace - 1)], g0_r)
    mine = gr0.at[pl.ds(core * nplace, nplace)]
    send(mine, mine, i_s, i_r, sibling)
    arrived(mine, i_r)
    nrows = ndp * 8
    groups = gr0[...].reshape(nrows, 128).astype(F32)
    member = jnp.where(groups == iota((nrows, 128), 1).astype(F32), 1.0, 0.0)
    member = jnp.transpose(member, (1, 0))[0:GROUPS]
    rr, col = iota((64, nrows), 0), iota((64, nrows), 1)
    a, zz = rr & 7, rr >> 3
    late = (a >= 3).astype(jnp.int32)
    source = 4 * (2 * (2 * zz + yh) + late) + (a - 3 * late)
    span = 4 * (2 * ((col >> 3) & (nplace - 1)) + col // (8 * nplace)) + ((col >> 1) & 3)
    pick = jnp.where((span == source) & (a < 6), 1.0, 0.0)
    cmat[...] = jnp.concatenate([member, pick], 0).astype(BF16)

    sent(hy, hy_s)
    sent(seven(hr), hz_s)
    sent(seven(pr), pr_s)
    sent(seven(sr), sr_s)
    sent(seven(lr), lr_s)
    sent(seven(rt.at[0]), rt_s)
    sent(py.at[0], py_s)
    sent(sy.at[0], sy_s)
    sent(ly.at[0], ly_s)
    sent(rt.at[0], ty_s)
    sent(gr0.at[pl.ds(0, nplace - 1)], g0_s)
    sent(mine, i_s)
    drain()

    arrived(rt.at[1 - yh], ty_r)
    r = iota((256, 256), 0)
    want = ((r >> 2) & 7) * 32 + (r >> 7) * 16 + ((r >> 5) & 3) * 4 + (r & 3)
    perm = jnp.where(iota((256, 256), 1) == want, 1.0, 0.0).astype(BF16)
    for y in range(2):
        tb[y] = dot(perm, rt[y].reshape(256, 128)).astype(BF16).reshape(2, 128, 128)

    ours = core * half
    arrived(gr.at[pl.ds(0, nplace - 1)], grn_r)
    block = gr.at[pl.ds(ours + yh * nplace, nplace)]
    send(block, block, fn_s, fn_r, sibling)
    arrived(gr.at[pl.ds(0, nplace)], grf_r)
    block = gr.at[pl.ds(ours + (1 - yh) * nplace, nplace)]
    send(block, block, ff_s, ff_r, sibling)

    hrows = nplace * 8
    jrow = iota((hrows, 128), 0) & 1

    def scored(first):
        value = jnp.zeros((hrows, 128), F32)
        for y in range(2):
            grads = gr[pl.ds(first + y * nplace, nplace)].reshape(hrows, 128)
            value += jnp.where(jrow == 0, dot(grads, tb[y, 0]), dot(grads, tb[y, 1]))
        one = value.astype(BF16)
        return one, (value - one.astype(F32)).astype(BF16)

    vals[0, pl.ds(core * hrows, hrows)], vals[1, pl.ds(core * hrows, hrows)] = scored(ours)

    arrived(block, fn_r)
    arrived(block, ff_r)

    theirs = (1 - core) * hrows
    vals[0, pl.ds(theirs, hrows)], vals[1, pl.ds(theirs, hrows)] = scored((1 - core) * half)
    c = cmat[...]
    summed = dot(c, vals[1]) + dot(c, vals[0])
    fg[...] = summed[0:GROUPS].astype(BF16)
    fs[...] = summed[GROUPS:].reshape(NZ, 8, 128)

    for k in range(1, NZ):
        o, device = at_z(k)
        send(fs.at[o], fsr.at[z], fs_s, fs_r, device)
        send(fg, fgr.at[z], fg_s, fg_r, device)
    fsr[z] = fs[z]
    fgr[z] = fg[...]

    sent(gr.at[pl.ds(0, half - 1)], gr_s)
    sent(block, fn_s)
    sent(block, ff_s)
    sent(seven(fsr), fs_s)
    sent(seven(fgr), fg_s)
    drain()

    arrived(seven(fsr), fs_r)
    arrived(seven(fgr), fg_r)

    for half in range(2):
        a, b = fsr[4 * half], fgr[4 * half].astype(F32)
        for k in range(4 * half + 1, 4 * half + 4):
            a, b = a + fsr[k], b + fgr[k].astype(F32)
        out_s[half] = a
        out_g[half] = b


def per_device(ndp, logits, labels, hidden, proj_in, proj_out, test_grads, group_ids):
    tokens, width = logits.shape
    any_spec = pl.BlockSpec(memory_space=pl.ANY)
    vmem = pl.BlockSpec(memory_space=pltpu.VMEM)
    dma, V = pltpu.SemaphoreType.DMA, pltpu.VMEM
    row_chunks = (96, 96)
    s, g = pl.pallas_call(
        functools.partial(kernel, ndp, row_chunks),
        name="scores",
        out_shape=(
            pltpu.VMEM((2, 8, 128), F32),
            pltpu.VMEM((2, GROUPS, 128), F32),
        ),
        in_specs=[any_spec] * 7,
        out_specs=(vmem, vmem),
        scratch_shapes=[
            V((tokens, width), BF16), V((RANK + 16, width), BF16), V((1, tokens), jnp.int32), V((1, 3), jnp.int32),
            V((tokens, 256), BF16), V((RANK, 256), BF16), V((128, 256), BF16),
            V((2, 48, 128), F32), V((2, 48, 128), BF16), V((48, 128), BF16), V((48, 128), BF16), V((NZ, 48, 128), BF16),
            V((NZ, 8, tokens), F32), V((NZ, 8, tokens), F32), V((2, 8, tokens), F32),
            V((2, tokens), F32), V((NZ, 2, tokens), F32), V((2, 2, tokens), F32),
            V((NZ, 8, tokens), BF16), V((NZ, 8, tokens), BF16), V((2, 8, tokens), BF16),
            V((NZ, 32, 128), BF16), V((2, NZ, 32, 128), BF16), V((2, 2, 128, 128), BF16),
            V((8, 128), BF16), V((ndp, 8, 128), BF16), V((8, 128), BF16), V((2 * ndp, 8, 128), BF16),
            V((96, ndp * 8), BF16), V((2, ndp * 8, 128), BF16),
            V((GROUPS, 128), BF16), V((NZ, GROUPS, 128), BF16), V((NZ, 8, 128), F32), V((NZ, 8, 128), F32),
            dma((6,)), dma((len(row_chunks),)),
            *[dma] * 35,
        ],
        compiler_params=pltpu.CompilerParams(collective_id=0, has_side_effects=True),
    )(
        logits, labels.reshape(1, tokens), hidden, proj_in.T, proj_out.T, test_grads,
        group_ids.reshape(1, 3),
    )
    return jnp.sum(s, axis=0)[0:6], jnp.sum(g, axis=0)


def solution(mesh):
    in_specs = (
        P("dp", "vocab"),
        P("dp"),
        P("dp", "vocab"),
        P("vocab", None),
        P("vocab", None),
        P("dp", "vocab"),
        P("dp"),
    )
    out_specs = (P("vocab", "dp"), P(None, "dp"))
    return jax.shard_map(
        functools.partial(per_device, mesh.shape["dp"]),
        mesh=mesh, in_specs=in_specs, out_specs=out_specs, check_vma=False,
    )
```

```python
import functools

import jax
import jax.numpy as jnp
from jax import lax
from jax.experimental import pallas as pl
from jax.experimental.pallas import tpu as pltpu
from jax.sharding import PartitionSpec as P

RANK = 64
SPAN = 64
GROUPS = 32
MESH = pl.DeviceIdType.MESH
F32 = jnp.float32
BF16 = jnp.bfloat16
NT = (((1,), (1,)), ((), ()))
NZ = 8
NX = 4
KBLOCK = 1024
EARLY = 5
Z_ORDER = (4, 3, 5, 2, 6, 1, 7)


def dot(a, b):
    return jnp.dot(a, b, preferred_element_type=F32)


def dot_nt(a, b):
    return lax.dot_general(a, b, NT, preferred_element_type=F32)


def iota(shape, dim):
    return lax.broadcasted_iota(jnp.int32, shape, dim)


def kernel(
    ndp, row_chunks,
    logits, labels, hidden, pin, pout, tgrads, gids,
    out_s, out_g,
    xv, wv, lab, gid, hid, pinv, tg,
    hp, hb, hy, hz, hr,
    ps, pr, py, st, sr, sy,
    ls, lr, ly,
    ts, rt, tb,
    gs0, gr0, gs, gr, cmat, vals,
    fs, fsr,
    lsem, xsem,
    hy_s, hy_r, hz_s, hz_r,
    pr_s, pr_r, py_s, py_r, sr_s, sr_r, sy_s, sy_r,
    lr_s, lr_r, ly_s, ly_r,
    rt_s, rt_r, ru_s, ru_r, ty_s, ty_r,
    g0_s, g0_r, i_s, i_r, gr_s, grn_r, grf_r, fn_s, fn_r, ff_s, ff_r,
    fs_s, fs_r,
    line_sem,
):
    dp = lax.axis_index("dp")
    v = lax.axis_index("vocab")
    z, yh = v // 2, v % 2
    tokens, width = logits.shape
    spans = tokens // SPAN
    vbase = v * width

    def at_z(k):
        other = lax.rem(z + k, NZ)
        return other, {"dp": dp, "vocab": other * 2 + yh}

    partner = {"dp": dp, "vocab": z * 2 + (1 - yh)}

    local = [
        pltpu.make_async_copy(src, dst, lsem.at[k])
        for k, (src, dst) in enumerate(
            [(pin, pinv), (hidden, hid), (tgrads, tg), (pout, wv.at[pl.ds(0, RANK)]), (labels, lab), (gids, gid)]
        )
    ]
    for copy in local[:3]:
        copy.start()
    rows_at = []
    at = 0
    for k, n in enumerate(row_chunks):
        copy = pltpu.make_async_copy(logits.at[pl.ds(at, n)], xv.at[pl.ds(at, n)], xsem.at[k])
        copy.start()
        if k == 0:
            local[3].start()
        rows_at.append((at, n, copy))
        at += n
    for copy in local[4:]:
        copy.start()

    barrier = pltpu.get_barrier_semaphore()

    core, place = lax.rem(dp, 2), dp // 2
    nplace = ndp // 2
    places = [lax.rem(place + nplace // 2 + k, nplace) for k in range(nplace) if k != nplace // 2]
    far = [{"dp": 2 * o + core, "vocab": z * 2 + (1 - yh)} for o in places] + [partner]
    near = [{"dp": 2 * o + core, "vocab": v} for o in places]
    sibling = {"dp": dp + 1 - 2 * core, "vocab": v}

    x, ylow = lax.rem(place, NX), place // NX
    ny = nplace // NX
    y_line = []
    for k in range(1, 2 * ny):
        o = lax.rem(yh * ny + ylow + ((k + ny - 1) % (2 * ny - 1) + 1), 2 * ny)
        y_line.append({"dp": (lax.rem(o, ny) * NX + x) * 2 + core, "vocab": z * 2 + o // ny})
    x_line = [{"dp": (ylow * NX + lax.rem(x + k, NX)) * 2 + core, "vocab": v} for k in range(1, NX)]

    for device in y_line + x_line + [sibling]:
        pl.semaphore_signal(barrier, inc=1, device_id=device, device_id_type=MESH)
    for k in range(1, NZ):
        pl.semaphore_signal(barrier, inc=1, device_id=at_z(k)[1], device_id_type=MESH)

    sends = []

    def send(src, dst, ssem, rsem, device):
        pltpu.make_async_remote_copy(
            src_ref=src, dst_ref=dst, send_sem=ssem, recv_sem=rsem, device_id=device, device_id_type=MESH
        ).start()

    def arrived(ref, sem):
        pltpu.make_async_remote_copy(
            src_ref=ref, dst_ref=ref, send_sem=sem, recv_sem=sem, device_id=partner, device_id_type=MESH
        ).wait_recv()

    def sent(ref, sem):
        sends.append((ref, sem))

    def drain():
        for ref, sem in sends:
            pltpu.make_async_remote_copy(
                src_ref=ref, dst_ref=ref, send_sem=sem, recv_sem=sem, device_id=partner, device_id_type=MESH
            ).wait_send()
        sends.clear()

    def seven(ref):
        return ref.at[pl.ds(0, NZ - 1)]

    wv[RANK : RANK + 16, :] = jnp.ones((16, width), BF16)
    local[0].wait()
    local[1].wait()
    r = iota((RANK, RANK), 0)
    want = ((r >> 2) & 7) * 8 + (r >> 5) * 4 + (r & 3)
    perm = jnp.where(iota((RANK, RANK), 1) == want, 1.0, 0.0).astype(BF16)
    pin_rows = dot(perm, pinv[...]).astype(BF16)
    h_part = dot_nt(pin_rows, hid[...])
    for y in range(2):
        side = h_part[32 * y : 32 * y + 32]
        hp[y, 0:32] = side[:, 0:128]
        hp[y, 32:48] = jnp.concatenate([side[0:16, 128:], side[16:, 128:]], 1)
    hb[...] = hp[...].astype(BF16)

    local[2].wait()
    r = iota((256, 256), 0)
    want = (r & 3) * 64 + (r >> 5) * 8 + ((r >> 2) & 3) * 2 + ((r >> 4) & 1)
    perm = jnp.where(iota((256, 256), 1) == want, 1.0, 0.0).astype(BF16)
    ts[yh] = dot_nt(perm, tg[...]).astype(BF16).reshape(NZ, 32, 128)
    whole = width // 128

    def top_of(at, n):
        rows = pl.ds(at, n)
        top = xv[rows, 0:128]
        for k in range(1, whole):
            top = jnp.maximum(top, xv[rows, k * 128 : (k + 1) * 128])
        top = jnp.max(top.astype(F32), axis=1, keepdims=True)
        if width % 128:
            rest = xv[rows, whole * 128 : width].astype(F32)
            top = jnp.maximum(top, jnp.max(rest, axis=1, keepdims=True))
        return top

    def product_of(at, n, top, los):
        acc = jnp.zeros((RANK + 16, n), F32)
        for lo in los:
            m = min(KBLOCK, width - lo)
            e = jnp.exp(xv[pl.ds(at, n), lo : lo + m].astype(F32) - top).astype(BF16)
            acc += dot_nt(wv[:, lo : lo + m], e)
        return acc

    def keep(at, n, top, acc):
        ps[:, :, at : at + n] = acc[0:RANK].reshape(NZ, 8, n)
        st[1:2, at : at + n] = acc[RANK : RANK + 1]
        st[0:1, at : at + n] = jnp.transpose(jnp.broadcast_to(top, (n, 128)), (1, 0))[0:1]

    los = list(range(0, width, KBLOCK))
    (at, n, copy), (at2, n2, copy2) = rows_at
    copy.wait()
    top = top_of(at, n)
    local[3].wait()
    acc = product_of(at, n, top, los[:EARLY])
    copy2.wait()
    acc += product_of(at, n, top, los[EARLY:])
    top2 = top_of(at2, n2)
    keep(at, n, top, acc)
    keep(at2, n2, top2, product_of(at2, n2, top2, los))

    pl.semaphore_wait(barrier, NZ - 1 + 2 * ny - 1 + NX - 1 + 1)

    send(hb.at[1 - yh], hy, hy_s, hy_r, partner)
    for k in Z_ORDER:
        o, device = at_z(k)
        send(ps.at[o], pr.at[z], pr_s, pr_r, device)
        send(st, sr.at[z], sr_s, sr_r, device)
    pr[z] = ps[z]
    sr[z] = st[...]

    local[4].wait()
    lab_row = lab[...] - vbase
    hot = jnp.where(iota((256, tokens), 0) == (lab_row & 255), 1.0, 0.0).astype(BF16)
    lab_block = lab_row >> 8
    label_rows = jnp.zeros((RANK, tokens), F32)
    blocks = width // 256
    for first in range(0, blocks, 8):
        some = range(first, min(first + 8, blocks))
        found = dot(jnp.concatenate([wv[0:RANK, 256 * k : 256 * k + 256] for k in some], 0), hot)
        for k in some:
            label_rows = jnp.where(lab_block == k, found[RANK * (k - first) : RANK * (k - first + 1)], label_rows)
    if width % 256:
        found = dot(wv[0:RANK, 256 * blocks : width], hot[0 : width % 256])
        label_rows = jnp.where(lab_block == blocks, found, label_rows)
    ls[...] = label_rows.reshape(NZ, 8, tokens).astype(BF16)
    for k in Z_ORDER:
        o, device = at_z(k)
        send(ls.at[o], lr.at[z], lr_s, lr_r, device)
    lr[z] = ls[z]
    send(ts.at[yh], ts.at[yh], ty_s, ty_r, partner)

    for device in y_line:
        pl.semaphore_signal(line_sem, inc=1, device_id=device, device_id_type=MESH)

    local[5].wait()
    srow = iota((8, 128), 0) >> 1
    ids = jnp.full((8, 128), -1, jnp.int32)
    for s in range(spans):
        ids = jnp.where(srow == s, jnp.broadcast_to(gid[0:1, s : s + 1], (8, 128)), ids)
    gs0[...] = ids.astype(F32).astype(BF16)


    arrived(hy, hy_r)
    hz[...] = (hp[yh] + hy[...].astype(F32)).astype(BF16)
    for k in Z_ORDER:
        o, device = at_z(k)
        send(hz, hr.at[z], hz_s, hz_r, device)
    hr[z] = hz[...]

    pl.semaphore_wait(line_sem, 2 * ny - 1)
    for o in places:
        send(gs0, gr0.at[core * nplace + place], g0_s, g0_r, {"dp": 2 * o + core, "vocab": v})
    gr0[core * nplace + place] = gs0[...]

    def merged(tops, totals, products):
        peak = tops[0]
        for t in tops[1:]:
            peak = jnp.maximum(peak, t)
        total = jnp.zeros_like(peak)
        product = jnp.zeros_like(products[0])
        for t, s, p in zip(tops, totals, products):
            w = jnp.exp(t - peak)
            total = total + w * s
            product = product + w * p
        return peak, total, product

    arrived(seven(pr), pr_r)
    arrived(seven(sr), sr_r)
    peak, total, product = merged(
        [sr[k, 0:1] for k in range(NZ)], [sr[k, 1:2] for k in range(NZ)], [pr[k] for k in range(NZ)]
    )
    py[yh] = product
    sy[yh, 0:1] = peak
    sy[yh, 1:2] = total
    send(py.at[yh], py.at[yh], py_s, py_r, partner)
    send(sy.at[yh], sy.at[yh], sy_s, sy_r, partner)

    arrived(seven(lr), lr_r)
    label_part = lr[0].astype(F32)
    for k in range(1, NZ):
        label_part = label_part + lr[k].astype(F32)
    ly[yh] = label_part.astype(BF16)
    send(ly.at[yh], ly.at[yh], ly_s, ly_r, partner)

    arrived(ts.at[1 - yh], ty_r)
    for k in Z_ORDER:
        o, device = at_z(k)
        for y in range(2):
            send(ts.at[y, o], rt.at[y, z], (rt_s, ru_s)[y], (rt_r, ru_r)[y], device)
    for y in range(2):
        rt[y, z] = ts[y, z]

    arrived(seven(hr), hz_r)
    packed = hr[0].astype(F32)
    for k in range(1, NZ):
        packed = packed + hr[k].astype(F32)
    hproj = jnp.concatenate(
        [packed[0:32], jnp.concatenate([packed[32:48, 0:64], packed[32:48, 64:]], 0)], 1
    )
    h_high = hproj.astype(BF16)
    h_low = (hproj - h_high.astype(F32)).astype(BF16)
    rhs = jnp.concatenate([h_high] * 4 + [h_low] * 4, 0)

    arrived(py.at[1 - yh], py_r)
    arrived(sy.at[1 - yh], sy_r)
    peak, total, product = merged(
        [sy[k, 0:1] for k in range(2)], [sy[k, 1:2] for k in range(2)], [py[k] for k in range(2)]
    )
    arrived(ly.at[1 - yh], ly_r)
    rproj = product / total - (ly[0].astype(F32) + ly[1].astype(F32))

    span_of = iota((8, tokens), 1) // SPAN
    high = rproj.astype(BF16).astype(F32)
    low = rproj - high
    lhs = [jnp.where(span_of == s, high, 0.0) for s in range(spans)]
    lhs += [jnp.where(span_of == s, low, 0.0) for s in range(spans)]
    outer = dot_nt(jnp.concatenate(lhs, 0).astype(BF16), rhs)
    outer = (outer[0 : 8 * spans, 128:] + outer[8 * spans :, 0:128]) + outer[0 : 8 * spans, 0:128]
    block = iota((8, 128), 1) // 32
    pair = iota((8, 128), 0) >> 1
    tile = jnp.zeros((8, 128), F32)
    for s in range(spans):
        a = outer[8 * s : 8 * s + 8]
        for jq in range(4):
            shift = (2 * s - 2 * jq) % 8
            moved = pltpu.roll(a, shift, 0) if shift else a
            tile = jnp.where((pair == s) & (block == jq), moved, tile)
    gs[...] = tile.astype(BF16)

    half = 2 * nplace
    me = core * half + yh * nplace + place
    for device in far:
        send(gs, gr.at[me], gr_s, grf_r, device)
    for device in near:
        send(gs, gr.at[me], gr_s, grn_r, device)
    gr[me] = gs[...]

    arrived(gr0.at[pl.ds(0, nplace - 1)], g0_r)
    mine = gr0.at[pl.ds(core * nplace, nplace)]
    send(mine, mine, i_s, i_r, sibling)
    arrived(mine, i_r)
    nrows = ndp * 8
    groups = gr0[...].reshape(nrows, 128).astype(F32)
    member = jnp.where(groups == iota((nrows, 128), 1).astype(F32), 1.0, 0.0)
    member = jnp.transpose(member, (1, 0))[0:GROUPS]
    rr, col = iota((64, nrows), 0), iota((64, nrows), 1)
    a, zz = rr & 7, rr >> 3
    late = (a >= 3).astype(jnp.int32)
    source = 4 * (2 * (2 * zz + yh) + late) + (a - 3 * late)
    span = 4 * (2 * ((col >> 3) & (nplace - 1)) + col // (8 * nplace)) + ((col >> 1) & 3)
    pick = jnp.where((span == source) & (a < 6), 1.0, 0.0)
    cmat[...] = jnp.concatenate([member, pick], 0).astype(BF16)

    sent(hy, hy_s)
    sent(seven(hr), hz_s)
    sent(seven(pr), pr_s)
    sent(seven(sr), sr_s)
    sent(seven(lr), lr_s)
    sent(seven(rt.at[0]), rt_s)
    sent(seven(rt.at[1]), ru_s)
    sent(py.at[0], py_s)
    sent(sy.at[0], sy_s)
    sent(ly.at[0], ly_s)
    sent(rt.at[0], ty_s)
    sent(gr0.at[pl.ds(0, nplace - 1)], g0_s)
    sent(mine, i_s)
    drain()

    for y in range(2):
        arrived(seven(rt.at[y]), (rt_r, ru_r)[y])
    r = iota((256, 256), 0)
    want = ((r >> 2) & 7) * 32 + (r >> 7) * 16 + ((r >> 5) & 3) * 4 + (r & 3)
    perm = jnp.where(iota((256, 256), 1) == want, 1.0, 0.0).astype(BF16)
    for y in range(2):
        tb[y] = dot(perm, rt[y].reshape(256, 128)).astype(BF16).reshape(2, 128, 128)

    arrived(gr.at[pl.ds(0, nplace - 1)], grn_r)
    nearby = gr.at[pl.ds(core * half + yh * nplace, nplace)]
    send(nearby, nearby, fn_s, fn_r, sibling)
    arrived(gr.at[pl.ds(0, nplace)], grf_r)
    distant = gr.at[pl.ds(core * half + (1 - yh) * nplace, nplace)]
    send(distant, distant, ff_s, ff_r, sibling)

    hrows = nplace * 8
    jrow = iota((hrows, 128), 0) & 1

    def scored(c, y):
        grads = gr[pl.ds(c * half + y * nplace, nplace)].reshape(hrows, 128)
        return jnp.where(jrow == 0, dot(grads, tb[y, 0]), dot(grads, tb[y, 1]))

    def split(value):
        one = value.astype(BF16)
        return one, (value - one.astype(F32)).astype(BF16)

    arrived(nearby, fn_r)
    vals[0, pl.ds(core * hrows, hrows)], vals[1, pl.ds(core * hrows, hrows)] = split(
        scored(core, 0) + scored(core, 1)
    )
    here = scored(1 - core, yh)

    arrived(distant, ff_r)

    theirs = (1 - core) * hrows
    vals[0, pl.ds(theirs, hrows)], vals[1, pl.ds(theirs, hrows)] = split(here + scored(1 - core, 1 - yh))
    c = cmat[...]
    summed = dot(c, vals[1]) + dot(c, vals[0])
    low = summed.astype(BF16)
    for o in range(NZ):
        fs[o, 0:GROUPS] = low[0:GROUPS]
        fs[o, GROUPS:] = low[GROUPS + 8 * o : GROUPS + 8 * o + 8]

    for k in Z_ORDER:
        o, device = at_z(k)
        send(fs.at[o], fsr.at[z], fs_s, fs_r, device)
    fsr[z] = fs[z]

    sent(gr.at[pl.ds(0, half - 1)], gr_s)
    sent(nearby, fn_s)
    sent(distant, ff_s)
    sent(seven(fsr), fs_s)
    drain()

    arrived(seven(fsr), fs_r)

    total = fsr[0].astype(F32)
    for k in range(1, NZ):
        total = total + fsr[k].astype(F32)
    out_s[...] = total[GROUPS : GROUPS + 6]
    out_g[...] = total[0:GROUPS]


def per_device(ndp, logits, labels, hidden, proj_in, proj_out, test_grads, group_ids):
    tokens, width = logits.shape
    any_spec = pl.BlockSpec(memory_space=pl.ANY)
    vmem = pl.BlockSpec(memory_space=pltpu.VMEM)
    dma, V = pltpu.SemaphoreType.DMA, pltpu.VMEM
    row_chunks = (96, 96)
    s, g = pl.pallas_call(
        functools.partial(kernel, ndp, row_chunks),
        name="scores",
        out_shape=(
            pltpu.VMEM((6, 128), F32),
            pltpu.VMEM((GROUPS, 128), F32),
        ),
        in_specs=[any_spec] * 7,
        out_specs=(vmem, vmem),
        scratch_shapes=[
            V((tokens, width), BF16), V((RANK + 16, width), BF16), V((1, tokens), jnp.int32), V((1, 3), jnp.int32),
            V((tokens, 256), BF16), V((RANK, 256), BF16), V((128, 256), BF16),
            V((2, 48, 128), F32), V((2, 48, 128), BF16), V((48, 128), BF16), V((48, 128), BF16), V((NZ, 48, 128), BF16),
            V((NZ, 8, tokens), F32), V((NZ, 8, tokens), F32), V((2, 8, tokens), F32),
            V((2, tokens), F32), V((NZ, 2, tokens), F32), V((2, 2, tokens), F32),
            V((NZ, 8, tokens), BF16), V((NZ, 8, tokens), BF16), V((2, 8, tokens), BF16),
            V((2, NZ, 32, 128), BF16), V((2, NZ, 32, 128), BF16), V((2, 2, 128, 128), BF16),
            V((8, 128), BF16), V((ndp, 8, 128), BF16), V((8, 128), BF16), V((2 * ndp, 8, 128), BF16),
            V((96, ndp * 8), BF16), V((2, ndp * 8, 128), BF16),
            V((NZ, GROUPS + 8, 128), BF16), V((NZ, GROUPS + 8, 128), BF16),
            dma((6,)), dma((len(row_chunks),)),
            *[dma] * 35, pltpu.SemaphoreType.REGULAR,
        ],
        compiler_params=pltpu.CompilerParams(collective_id=0, has_side_effects=True),
    )(
        logits, labels.reshape(1, tokens), hidden, proj_in.T, proj_out.T, test_grads,
        group_ids.reshape(1, 3),
    )
    return s, g


def solution(mesh):
    in_specs = (
        P("dp", "vocab"),
        P("dp"),
        P("dp", "vocab"),
        P("vocab", None),
        P("vocab", None),
        P("dp", "vocab"),
        P("dp"),
    )
    out_specs = (P("vocab", "dp"), P(None, "dp"))
    return jax.shard_map(
        functools.partial(per_device, mesh.shape["dp"]),
        mesh=mesh, in_specs=in_specs, out_specs=out_specs, check_vma=False,
    )
```

```python
import functools

import jax
import jax.numpy as jnp
from jax import lax
from jax.experimental import pallas as pl
from jax.experimental.pallas import tpu as pltpu
from jax.sharding import PartitionSpec as P

RANK = 64
SPAN = 64
GROUPS = 32
MESH = pl.DeviceIdType.MESH
F32 = jnp.float32
BF16 = jnp.bfloat16
NT = (((1,), (1,)), ((), ()))
NZ = 8
NX = 4
KBLOCK = 1024
EARLY = 5
Z_ORDER = (4, 3, 5, 2, 6, 1, 7)


def dot(a, b):
    return jnp.dot(a, b, preferred_element_type=F32)


def dot_nt(a, b):
    return lax.dot_general(a, b, NT, preferred_element_type=F32)


def iota(shape, dim):
    return lax.broadcasted_iota(jnp.int32, shape, dim)


def kernel(
    ndp, row_chunks,
    logits, labels, hidden, pin, pout, tgrads, gids,
    out_s, out_g,
    xv, wv, lab, gid, hid, pinv, tg,
    hp, hb, hy, hz, hr,
    ps, pr, py, st, sr, sy,
    ls, lr, ly,
    ts, rt, tb,
    gs0, gr0, gs, gr, cmat, vals,
    fs, fsr,
    lsem, xsem,
    hy_s, hy_r, hz_s, hz_r,
    pr_s, pr_r, py_s, py_r, sr_s, sr_r, sy_s, sy_r,
    lr_s, lr_r, ly_s, ly_r,
    rt_s, rt_r, ru_s, ru_r, ty_s, ty_r,
    g0_s, g0_r, i_s, i_r, gr_s, grn_r, grf_r, fn_s, fn_r, ff_s, ff_r,
    fs_s, fs_r,
    line_sem,
):
    dp = lax.axis_index("dp")
    v = lax.axis_index("vocab")
    z, yh = v // 2, v % 2
    tokens, width = logits.shape
    spans = tokens // SPAN
    vbase = v * width

    def at_z(k):
        other = lax.rem(z + k, NZ)
        return other, {"dp": dp, "vocab": other * 2 + yh}

    partner = {"dp": dp, "vocab": z * 2 + (1 - yh)}

    local = [
        pltpu.make_async_copy(src, dst, lsem.at[k])
        for k, (src, dst) in enumerate(
            [(pin, pinv), (hidden, hid), (tgrads, tg), (pout, wv.at[pl.ds(0, RANK)]), (labels, lab), (gids, gid)]
        )
    ]
    for copy in local[:3]:
        copy.start()
    rows_at = []
    at = 0
    for k, n in enumerate(row_chunks):
        copy = pltpu.make_async_copy(logits.at[pl.ds(at, n)], xv.at[pl.ds(at, n)], xsem.at[k])
        copy.start()
        if k == 0:
            local[3].start()
        rows_at.append((at, n, copy))
        at += n
    for copy in local[4:]:
        copy.start()

    barrier = pltpu.get_barrier_semaphore()

    core, place = lax.rem(dp, 2), dp // 2
    nplace = ndp // 2
    places = [lax.rem(place + nplace // 2 + k, nplace) for k in range(nplace) if k != nplace // 2]
    far = [{"dp": 2 * o + core, "vocab": z * 2 + (1 - yh)} for o in places] + [partner]
    near = [{"dp": 2 * o + core, "vocab": v} for o in places]
    sibling = {"dp": dp + 1 - 2 * core, "vocab": v}

    x, ylow = lax.rem(place, NX), place // NX
    ny = nplace // NX
    y_line = []
    for k in range(1, 2 * ny):
        o = lax.rem(yh * ny + ylow + ((k + ny - 1) % (2 * ny - 1) + 1), 2 * ny)
        y_line.append({"dp": (lax.rem(o, ny) * NX + x) * 2 + core, "vocab": z * 2 + o // ny})
    x_line = [{"dp": (ylow * NX + lax.rem(x + k, NX)) * 2 + core, "vocab": v} for k in range(1, NX)]

    for device in y_line + x_line + [sibling]:
        pl.semaphore_signal(barrier, inc=1, device_id=device, device_id_type=MESH)
    for k in range(1, NZ):
        pl.semaphore_signal(barrier, inc=1, device_id=at_z(k)[1], device_id_type=MESH)

    sends = []

    def send(src, dst, ssem, rsem, device):
        pltpu.make_async_remote_copy(
            src_ref=src, dst_ref=dst, send_sem=ssem, recv_sem=rsem, device_id=device, device_id_type=MESH
        ).start()

    def arrived(ref, sem):
        pltpu.make_async_remote_copy(
            src_ref=ref, dst_ref=ref, send_sem=sem, recv_sem=sem, device_id=partner, device_id_type=MESH
        ).wait_recv()

    def sent(ref, sem):
        sends.append((ref, sem))

    def drain():
        for ref, sem in sends:
            pltpu.make_async_remote_copy(
                src_ref=ref, dst_ref=ref, send_sem=sem, recv_sem=sem, device_id=partner, device_id_type=MESH
            ).wait_send()
        sends.clear()

    def seven(ref):
        return ref.at[pl.ds(0, NZ - 1)]

    wv[RANK : RANK + 16, :] = jnp.ones((16, width), BF16)
    local[0].wait()
    local[1].wait()
    r = iota((RANK, RANK), 0)
    want = ((r >> 2) & 7) * 8 + (r >> 5) * 4 + (r & 3)
    perm = jnp.where(iota((RANK, RANK), 1) == want, 1.0, 0.0).astype(BF16)
    pin_rows = dot(perm, pinv[...]).astype(BF16)
    h_part = dot_nt(pin_rows, hid[...])
    for y in range(2):
        side = h_part[32 * y : 32 * y + 32]
        hp[y, 0:32] = side[:, 0:128]
        hp[y, 32:48] = jnp.concatenate([side[0:16, 128:], side[16:, 128:]], 1)
    hb[...] = hp[...].astype(BF16)

    local[2].wait()
    r = iota((256, 256), 0)
    want = (r & 3) * 64 + (r >> 5) * 8 + ((r >> 2) & 3) * 2 + ((r >> 4) & 1)
    perm = jnp.where(iota((256, 256), 1) == want, 1.0, 0.0).astype(BF16)
    ts[yh] = dot_nt(perm, tg[...]).astype(BF16).reshape(NZ, 32, 128)
    whole = width // 128

    def top_of(at, n):
        rows = pl.ds(at, n)
        top = xv[rows, 0:128]
        for k in range(1, whole):
            top = jnp.maximum(top, xv[rows, k * 128 : (k + 1) * 128])
        top = jnp.max(top.astype(F32), axis=1, keepdims=True)
        if width % 128:
            rest = xv[rows, whole * 128 : width].astype(F32)
            top = jnp.maximum(top, jnp.max(rest, axis=1, keepdims=True))
        return top

    def product_of(at, n, top, los):
        acc = jnp.zeros((RANK + 16, n), F32)
        for lo in los:
            m = min(KBLOCK, width - lo)
            e = jnp.exp(xv[pl.ds(at, n), lo : lo + m].astype(F32) - top).astype(BF16)
            acc += dot_nt(wv[:, lo : lo + m], e)
        return acc

    def keep(at, n, top, acc):
        ps[:, :, at : at + n] = acc[0:RANK].reshape(NZ, 8, n)
        st[1:2, at : at + n] = acc[RANK : RANK + 1]
        st[0:1, at : at + n] = jnp.transpose(jnp.broadcast_to(top, (n, 128)), (1, 0))[0:1]

    los = list(range(0, width, KBLOCK))
    (at, n, copy), (at2, n2, copy2) = rows_at
    copy.wait()
    top = top_of(at, n)
    local[3].wait()
    acc = product_of(at, n, top, los[:EARLY])
    copy2.wait()
    acc += product_of(at, n, top, los[EARLY:])
    top2 = top_of(at2, n2)
    keep(at, n, top, acc)
    keep(at2, n2, top2, product_of(at2, n2, top2, los))

    pl.semaphore_wait(barrier, NZ - 1 + 2 * ny - 1 + NX - 1 + 1)

    send(hb.at[1 - yh], hy, hy_s, hy_r, partner)
    for k in Z_ORDER:
        o, device = at_z(k)
        send(ps.at[o], pr.at[z], pr_s, pr_r, device)
        send(st, sr.at[z], sr_s, sr_r, device)
    pr[z] = ps[z]
    sr[z] = st[...]

    local[4].wait()
    lab_row = lab[...] - vbase
    hot = jnp.where(iota((256, tokens), 0) == (lab_row & 255), 1.0, 0.0).astype(BF16)
    lab_block = lab_row >> 8
    label_rows = jnp.zeros((RANK, tokens), F32)
    blocks = width // 256
    for first in range(0, blocks, 8):
        some = range(first, min(first + 8, blocks))
        found = dot(jnp.concatenate([wv[0:RANK, 256 * k : 256 * k + 256] for k in some], 0), hot)
        for k in some:
            label_rows = jnp.where(lab_block == k, found[RANK * (k - first) : RANK * (k - first + 1)], label_rows)
    if width % 256:
        found = dot(wv[0:RANK, 256 * blocks : width], hot[0 : width % 256])
        label_rows = jnp.where(lab_block == blocks, found, label_rows)
    ls[...] = label_rows.reshape(NZ, 8, tokens).astype(BF16)
    for k in Z_ORDER:
        o, device = at_z(k)
        send(ls.at[o], lr.at[z], lr_s, lr_r, device)
    lr[z] = ls[z]
    send(ts.at[yh], ts.at[yh], ty_s, ty_r, partner)

    for device in y_line:
        pl.semaphore_signal(line_sem, inc=1, device_id=device, device_id_type=MESH)

    local[5].wait()
    srow = iota((8, 128), 0) >> 1
    ids = jnp.full((8, 128), -1, jnp.int32)
    for s in range(spans):
        ids = jnp.where(srow == s, jnp.broadcast_to(gid[0:1, s : s + 1], (8, 128)), ids)
    gs0[...] = ids.astype(F32).astype(BF16)


    arrived(hy, hy_r)
    hz[...] = (hp[yh] + hy[...].astype(F32)).astype(BF16)
    for k in Z_ORDER:
        o, device = at_z(k)
        send(hz, hr.at[z], hz_s, hz_r, device)
    hr[z] = hz[...]

    pl.semaphore_wait(line_sem, 2 * ny - 1)
    for o in places:
        send(gs0, gr0.at[core * nplace + place], g0_s, g0_r, {"dp": 2 * o + core, "vocab": v})
    gr0[core * nplace + place] = gs0[...]

    def merged(tops, totals, products):
        peak = tops[0]
        for t in tops[1:]:
            peak = jnp.maximum(peak, t)
        total = jnp.zeros_like(peak)
        product = jnp.zeros_like(products[0])
        for t, s, p in zip(tops, totals, products):
            w = jnp.exp(t - peak)
            total = total + w * s
            product = product + w * p
        return peak, total, product

    arrived(seven(pr), pr_r)
    arrived(seven(sr), sr_r)
    peak, total, product = merged(
        [sr[k, 0:1] for k in range(NZ)], [sr[k, 1:2] for k in range(NZ)], [pr[k] for k in range(NZ)]
    )
    py[yh] = product
    sy[yh, 0:1] = peak
    sy[yh, 1:2] = total
    send(py.at[yh], py.at[yh], py_s, py_r, partner)
    send(sy.at[yh], sy.at[yh], sy_s, sy_r, partner)

    arrived(seven(lr), lr_r)
    label_part = lr[0].astype(F32)
    for k in range(1, NZ):
        label_part = label_part + lr[k].astype(F32)
    ly[yh] = label_part.astype(BF16)
    send(ly.at[yh], ly.at[yh], ly_s, ly_r, partner)

    arrived(seven(hr), hz_r)
    packed = hr[0].astype(F32)
    for k in range(1, NZ):
        packed = packed + hr[k].astype(F32)
    hproj = jnp.concatenate(
        [packed[0:32], jnp.concatenate([packed[32:48, 0:64], packed[32:48, 64:]], 0)], 1
    )
    h_high = hproj.astype(BF16)
    h_low = (hproj - h_high.astype(F32)).astype(BF16)
    rhs = jnp.concatenate([h_high] * 4 + [h_low] * 4, 0)

    arrived(ts.at[1 - yh], ty_r)
    for k in Z_ORDER:
        o, device = at_z(k)
        for y in range(2):
            send(ts.at[y, o], rt.at[y, z], (rt_s, ru_s)[y], (rt_r, ru_r)[y], device)
    for y in range(2):
        rt[y, z] = ts[y, z]

    arrived(py.at[1 - yh], py_r)
    arrived(sy.at[1 - yh], sy_r)
    peak, total, product = merged(
        [sy[k, 0:1] for k in range(2)], [sy[k, 1:2] for k in range(2)], [py[k] for k in range(2)]
    )
    arrived(ly.at[1 - yh], ly_r)
    rproj = product / total - (ly[0].astype(F32) + ly[1].astype(F32))

    span_of = iota((8, tokens), 1) // SPAN
    high = rproj.astype(BF16).astype(F32)
    low = rproj - high
    lhs = [jnp.where(span_of == s, high, 0.0) for s in range(spans)]
    lhs += [jnp.where(span_of == s, low, 0.0) for s in range(spans)]
    outer = dot_nt(jnp.concatenate(lhs, 0).astype(BF16), rhs)
    outer = (outer[0 : 8 * spans, 128:] + outer[8 * spans :, 0:128]) + outer[0 : 8 * spans, 0:128]
    block = iota((8, 128), 1) // 32
    pair = iota((8, 128), 0) >> 1
    tile = jnp.zeros((8, 128), F32)
    for s in range(spans):
        a = outer[8 * s : 8 * s + 8]
        for jq in range(4):
            shift = (2 * s - 2 * jq) % 8
            moved = pltpu.roll(a, shift, 0) if shift else a
            tile = jnp.where((pair == s) & (block == jq), moved, tile)
    gs[...] = tile.astype(BF16)

    half = 2 * nplace
    me = core * half + yh * nplace + place
    for device in far:
        send(gs, gr.at[me], gr_s, grf_r, device)
    for device in near:
        send(gs, gr.at[me], gr_s, grn_r, device)
    gr[me] = gs[...]

    arrived(gr0.at[pl.ds(0, nplace - 1)], g0_r)
    mine = gr0.at[pl.ds(core * nplace, nplace)]
    send(mine, mine, i_s, i_r, sibling)
    arrived(mine, i_r)
    nrows = ndp * 8
    groups = gr0[...].reshape(nrows, 128).astype(F32)
    member = jnp.where(groups == iota((nrows, 128), 1).astype(F32), 1.0, 0.0)
    member = jnp.transpose(member, (1, 0))[0:GROUPS]
    rr, col = iota((64, nrows), 0), iota((64, nrows), 1)
    a, zz = rr & 7, rr >> 3
    late = (a >= 3).astype(jnp.int32)
    source = 4 * (2 * (2 * zz + yh) + late) + (a - 3 * late)
    span = 4 * (2 * ((col >> 3) & (nplace - 1)) + col // (8 * nplace)) + ((col >> 1) & 3)
    pick = jnp.where((span == source) & (a < 6), 1.0, 0.0)
    cmat[...] = jnp.concatenate([member, pick], 0).astype(BF16)

    sent(hy, hy_s)
    sent(seven(hr), hz_s)
    sent(seven(pr), pr_s)
    sent(seven(sr), sr_s)
    sent(seven(lr), lr_s)
    sent(seven(rt.at[0]), rt_s)
    sent(seven(rt.at[1]), ru_s)
    sent(py.at[0], py_s)
    sent(sy.at[0], sy_s)
    sent(ly.at[0], ly_s)
    sent(rt.at[0], ty_s)
    sent(gr0.at[pl.ds(0, nplace - 1)], g0_s)
    sent(mine, i_s)
    drain()

    for y in range(2):
        arrived(seven(rt.at[y]), (rt_r, ru_r)[y])
    r = iota((256, 256), 0)
    want = ((r >> 2) & 7) * 32 + (r >> 7) * 16 + ((r >> 5) & 3) * 4 + (r & 3)
    perm = jnp.where(iota((256, 256), 1) == want, 1.0, 0.0).astype(BF16)
    for y in range(2):
        tb[y] = dot(perm, rt[y].reshape(256, 128)).astype(BF16).reshape(2, 128, 128)

    arrived(gr.at[pl.ds(0, nplace - 1)], grn_r)
    nearby = gr.at[pl.ds(core * half + yh * nplace, nplace)]
    send(nearby, nearby, fn_s, fn_r, sibling)
    arrived(gr.at[pl.ds(0, nplace)], grf_r)
    distant = gr.at[pl.ds(core * half + (1 - yh) * nplace, nplace)]
    send(distant, distant, ff_s, ff_r, sibling)

    hrows = nplace * 8
    jrow = iota((hrows, 128), 0) & 1

    def scored(c, y):
        grads = gr[pl.ds(c * half + y * nplace, nplace)].reshape(hrows, 128)
        return jnp.where(jrow == 0, dot(grads, tb[y, 0]), dot(grads, tb[y, 1]))

    def split(value):
        one = value.astype(BF16)
        return one, (value - one.astype(F32)).astype(BF16)

    arrived(nearby, fn_r)
    vals[0, pl.ds(core * hrows, hrows)], vals[1, pl.ds(core * hrows, hrows)] = split(
        scored(core, 0) + scored(core, 1)
    )
    here = scored(1 - core, yh)

    arrived(distant, ff_r)

    theirs = (1 - core) * hrows
    vals[0, pl.ds(theirs, hrows)], vals[1, pl.ds(theirs, hrows)] = split(here + scored(1 - core, 1 - yh))
    c = cmat[...]
    summed = dot(c, vals[1]) + dot(c, vals[0])
    low = summed.astype(BF16)
    for o in range(NZ):
        fs[o, 0:GROUPS] = low[0:GROUPS]
        fs[o, GROUPS:] = low[GROUPS + 8 * o : GROUPS + 8 * o + 8]

    for k in Z_ORDER:
        o, device = at_z(k)
        send(fs.at[o], fsr.at[z], fs_s, fs_r, device)
    fsr[z] = fs[z]

    sent(gr.at[pl.ds(0, half - 1)], gr_s)
    sent(nearby, fn_s)
    sent(distant, ff_s)
    sent(seven(fsr), fs_s)
    drain()

    arrived(seven(fsr), fs_r)

    total = fsr[0].astype(F32)
    for k in range(1, NZ):
        total = total + fsr[k].astype(F32)
    out_s[...] = total[GROUPS : GROUPS + 6]
    out_g[...] = total[0:GROUPS]


def per_device(ndp, logits, labels, hidden, proj_in, proj_out, test_grads, group_ids):
    tokens, width = logits.shape
    any_spec = pl.BlockSpec(memory_space=pl.ANY)
    vmem = pl.BlockSpec(memory_space=pltpu.VMEM)
    dma, V = pltpu.SemaphoreType.DMA, pltpu.VMEM
    row_chunks = (96, 96)
    s, g = pl.pallas_call(
        functools.partial(kernel, ndp, row_chunks),
        name="scores",
        out_shape=(
            pltpu.VMEM((6, 128), F32),
            pltpu.VMEM((GROUPS, 128), F32),
        ),
        in_specs=[any_spec] * 7,
        out_specs=(vmem, vmem),
        scratch_shapes=[
            V((tokens, width), BF16), V((RANK + 16, width), BF16), V((1, tokens), jnp.int32), V((1, 3), jnp.int32),
            V((tokens, 256), BF16), V((RANK, 256), BF16), V((128, 256), BF16),
            V((2, 48, 128), F32), V((2, 48, 128), BF16), V((48, 128), BF16), V((48, 128), BF16), V((NZ, 48, 128), BF16),
            V((NZ, 8, tokens), F32), V((NZ, 8, tokens), F32), V((2, 8, tokens), F32),
            V((2, tokens), F32), V((NZ, 2, tokens), F32), V((2, 2, tokens), F32),
            V((NZ, 8, tokens), BF16), V((NZ, 8, tokens), BF16), V((2, 8, tokens), BF16),
            V((2, NZ, 32, 128), BF16), V((2, NZ, 32, 128), BF16), V((2, 2, 128, 128), BF16),
            V((8, 128), BF16), V((ndp, 8, 128), BF16), V((8, 128), BF16), V((2 * ndp, 8, 128), BF16),
            V((96, ndp * 8), BF16), V((2, ndp * 8, 128), BF16),
            V((NZ, GROUPS + 8, 128), BF16), V((NZ, GROUPS + 8, 128), BF16),
            dma((6,)), dma((len(row_chunks),)),
            *[dma] * 35, pltpu.SemaphoreType.REGULAR,
        ],
        compiler_params=pltpu.CompilerParams(collective_id=0, has_side_effects=True),
    )(
        logits, labels.reshape(1, tokens), hidden, proj_in.T, proj_out.T, test_grads,
        group_ids.reshape(1, 3),
    )
    return s, g


def solution(mesh):
    in_specs = (
        P("dp", "vocab"),
        P("dp"),
        P("dp", "vocab"),
        P("vocab", None),
        P("vocab", None),
        P("dp", "vocab"),
        P("dp"),
    )
    out_specs = (P("vocab", "dp"), P(None, "dp"))
    return jax.shard_map(
        functools.partial(per_device, mesh.shape["dp"]),
        mesh=mesh, in_specs=in_specs, out_specs=out_specs, check_vma=False,
    )
```

```python
import functools

import jax
import jax.numpy as jnp
from jax import lax
from jax.experimental import pallas as pl
from jax.experimental.pallas import tpu as pltpu
from jax.sharding import PartitionSpec as P

RANK = 64
SPAN = 64
GROUPS = 32
MESH = pl.DeviceIdType.MESH
F32 = jnp.float32
BF16 = jnp.bfloat16
NT = (((1,), (1,)), ((), ()))
NZ = 8
NX = 4
KBLOCK = 1024
EARLY = 5
Z_ORDER = (4, 3, 5, 2, 6, 1, 7)


def dot(a, b):
    return jnp.dot(a, b, preferred_element_type=F32)


def dot_nt(a, b):
    return lax.dot_general(a, b, NT, preferred_element_type=F32)


def iota(shape, dim):
    return lax.broadcasted_iota(jnp.int32, shape, dim)


def kernel(
    ndp, row_chunks,
    logits, labels, hidden, pin, pout, tgrads, gids,
    out_s, out_g,
    xv, wv, lab, gid, hid, pinv, tg,
    hp, hb, hy, hz, hr,
    ps, pr, py, st, sr, sy,
    ls, lr, ly,
    ts, rt, tb,
    gs0, gr0, gs, gr, cmat, vals,
    fs, fsr,
    lsem, xsem,
    hy_s, hy_r, hz_s, hz_r,
    pr_s, pr_r, py_s, py_r, sr_s, sr_r, sy_s, sy_r,
    lr_s, lr_r, ly_s, ly_r,
    rt_s, rt_r, ru_s, ru_r, ty_s, ty_r,
    g0_s, g0_r, i_s, i_r, gr_s, grn_r, grf_r, fn_s, fn_r, ff_s, ff_r,
    fs_s, fs_r,
    line_sem,
):
    dp = lax.axis_index("dp")
    v = lax.axis_index("vocab")
    z, yh = v // 2, v % 2
    tokens, width = logits.shape
    spans = tokens // SPAN
    vbase = v * width

    def at_z(k):
        other = lax.rem(z + k, NZ)
        return other, {"dp": dp, "vocab": other * 2 + yh}

    partner = {"dp": dp, "vocab": z * 2 + (1 - yh)}

    local = [
        pltpu.make_async_copy(src, dst, lsem.at[k])
        for k, (src, dst) in enumerate(
            [(pin, pinv), (hidden, hid), (tgrads, tg), (pout, wv.at[pl.ds(0, RANK)]), (labels, lab), (gids, gid)]
        )
    ]
    for copy in local[:3]:
        copy.start()
    rows_at = []
    at = 0
    for k, n in enumerate(row_chunks):
        copy = pltpu.make_async_copy(logits.at[pl.ds(at, n)], xv.at[pl.ds(at, n)], xsem.at[k])
        copy.start()
        if k == 0:
            local[3].start()
        rows_at.append((at, n, copy))
        at += n
    for copy in local[4:]:
        copy.start()

    barrier = pltpu.get_barrier_semaphore()

    core, place = lax.rem(dp, 2), dp // 2
    nplace = ndp // 2
    places = [lax.rem(place + nplace // 2 + k, nplace) for k in range(nplace) if k != nplace // 2]
    far = [{"dp": 2 * o + core, "vocab": z * 2 + (1 - yh)} for o in places] + [partner]
    near = [{"dp": 2 * o + core, "vocab": v} for o in places]
    sibling = {"dp": dp + 1 - 2 * core, "vocab": v}

    x, ylow = lax.rem(place, NX), place // NX
    ny = nplace // NX
    y_line = []
    for k in range(1, 2 * ny):
        o = lax.rem(yh * ny + ylow + ((k + ny - 1) % (2 * ny - 1) + 1), 2 * ny)
        y_line.append({"dp": (lax.rem(o, ny) * NX + x) * 2 + core, "vocab": z * 2 + o // ny})
    x_line = [{"dp": (ylow * NX + lax.rem(x + k, NX)) * 2 + core, "vocab": v} for k in range(1, NX)]

    for device in y_line + x_line + [sibling]:
        pl.semaphore_signal(barrier, inc=1, device_id=device, device_id_type=MESH)
    for k in range(1, NZ):
        pl.semaphore_signal(barrier, inc=1, device_id=at_z(k)[1], device_id_type=MESH)

    sends = []

    def send(src, dst, ssem, rsem, device):
        pltpu.make_async_remote_copy(
            src_ref=src, dst_ref=dst, send_sem=ssem, recv_sem=rsem, device_id=device, device_id_type=MESH
        ).start()

    def arrived(ref, sem):
        pltpu.make_async_remote_copy(
            src_ref=ref, dst_ref=ref, send_sem=sem, recv_sem=sem, device_id=partner, device_id_type=MESH
        ).wait_recv()

    def sent(ref, sem):
        sends.append((ref, sem))

    def drain():
        for ref, sem in sends:
            pltpu.make_async_remote_copy(
                src_ref=ref, dst_ref=ref, send_sem=sem, recv_sem=sem, device_id=partner, device_id_type=MESH
            ).wait_send()
        sends.clear()

    def seven(ref):
        return ref.at[pl.ds(0, NZ - 1)]

    wv[RANK : RANK + 16, :] = jnp.ones((16, width), BF16)
    local[0].wait()
    local[1].wait()
    r = iota((RANK, RANK), 0)
    want = ((r >> 2) & 7) * 8 + (r >> 5) * 4 + (r & 3)
    perm = jnp.where(iota((RANK, RANK), 1) == want, 1.0, 0.0).astype(BF16)
    pin_rows = dot(perm, pinv[...]).astype(BF16)
    h_part = dot_nt(pin_rows, hid[...])
    for y in range(2):
        side = h_part[32 * y : 32 * y + 32]
        hp[y, 0:32] = side[:, 0:128]
        hp[y, 32:48] = jnp.concatenate([side[0:16, 128:], side[16:, 128:]], 1)
    hb[...] = hp[...].astype(BF16)

    local[2].wait()
    r = iota((256, 256), 0)
    want = (r & 3) * 64 + (r >> 5) * 8 + ((r >> 2) & 3) * 2 + ((r >> 4) & 1)
    perm = jnp.where(iota((256, 256), 1) == want, 1.0, 0.0).astype(BF16)
    ts[yh] = dot_nt(perm, tg[...]).astype(BF16).reshape(NZ, 32, 128)
    whole = width // 128

    def top_of(at, n):
        rows = pl.ds(at, n)
        top = xv[rows, 0:128]
        for k in range(1, whole):
            top = jnp.maximum(top, xv[rows, k * 128 : (k + 1) * 128])
        top = jnp.max(top.astype(F32), axis=1, keepdims=True)
        if width % 128:
            rest = xv[rows, whole * 128 : width].astype(F32)
            top = jnp.maximum(top, jnp.max(rest, axis=1, keepdims=True))
        return top

    def product_of(at, n, top, los):
        acc = jnp.zeros((RANK + 16, n), F32)
        for lo in los:
            m = min(KBLOCK, width - lo)
            e = jnp.exp(xv[pl.ds(at, n), lo : lo + m].astype(F32) - top).astype(BF16)
            acc += dot_nt(wv[:, lo : lo + m], e)
        return acc

    def keep(at, n, top, acc):
        ps[:, :, at : at + n] = acc[0:RANK].reshape(NZ, 8, n)
        st[1:2, at : at + n] = acc[RANK : RANK + 1]
        st[0:1, at : at + n] = jnp.transpose(jnp.broadcast_to(top, (n, 128)), (1, 0))[0:1]

    los = list(range(0, width, KBLOCK))
    (at, n, copy), (at2, n2, copy2) = rows_at
    copy.wait()
    top = top_of(at, n)
    local[3].wait()
    acc = product_of(at, n, top, los[:EARLY])
    copy2.wait()
    acc += product_of(at, n, top, los[EARLY:])
    top2 = top_of(at2, n2)
    keep(at, n, top, acc)
    keep(at2, n2, top2, product_of(at2, n2, top2, los))

    pl.semaphore_wait(barrier, NZ - 1 + 2 * ny - 1 + NX - 1 + 1)

    send(hb.at[1 - yh], hy, hy_s, hy_r, partner)
    for k in Z_ORDER:
        o, device = at_z(k)
        send(ps.at[o], pr.at[z], pr_s, pr_r, device)
        send(st, sr.at[z], sr_s, sr_r, device)
    pr[z] = ps[z]
    sr[z] = st[...]

    local[4].wait()
    lab_row = lab[...] - vbase
    hot = jnp.where(iota((256, tokens), 0) == (lab_row & 255), 1.0, 0.0).astype(BF16)
    lab_block = lab_row >> 8
    label_rows = jnp.zeros((RANK, tokens), F32)
    blocks = width // 256
    for first in range(0, blocks, 8):
        some = range(first, min(first + 8, blocks))
        found = dot(jnp.concatenate([wv[0:RANK, 256 * k : 256 * k + 256] for k in some], 0), hot)
        for k in some:
            label_rows = jnp.where(lab_block == k, found[RANK * (k - first) : RANK * (k - first + 1)], label_rows)
    if width % 256:
        found = dot(wv[0:RANK, 256 * blocks : width], hot[0 : width % 256])
        label_rows = jnp.where(lab_block == blocks, found, label_rows)
    ls[...] = label_rows.reshape(NZ, 8, tokens).astype(BF16)
    for k in Z_ORDER:
        o, device = at_z(k)
        send(ls.at[o], lr.at[z], lr_s, lr_r, device)
    lr[z] = ls[z]
    send(ts.at[yh], ts.at[yh], ty_s, ty_r, partner)

    for device in y_line:
        pl.semaphore_signal(line_sem, inc=1, device_id=device, device_id_type=MESH)

    local[5].wait()
    srow = iota((8, 128), 0) >> 1
    ids = jnp.full((8, 128), -1, jnp.int32)
    for s in range(spans):
        ids = jnp.where(srow == s, jnp.broadcast_to(gid[0:1, s : s + 1], (8, 128)), ids)
    gs0[...] = ids.astype(F32).astype(BF16)


    arrived(hy, hy_r)
    hz[...] = (hp[yh] + hy[...].astype(F32)).astype(BF16)
    for k in Z_ORDER:
        o, device = at_z(k)
        send(hz, hr.at[z], hz_s, hz_r, device)
    hr[z] = hz[...]

    pl.semaphore_wait(line_sem, 2 * ny - 1)
    for o in places:
        send(gs0, gr0.at[core * nplace + place], g0_s, g0_r, {"dp": 2 * o + core, "vocab": v})
    gr0[core * nplace + place] = gs0[...]

    def merged(tops, totals, products):
        peak = tops[0]
        for t in tops[1:]:
            peak = jnp.maximum(peak, t)
        total = jnp.zeros_like(peak)
        product = jnp.zeros_like(products[0])
        for t, s, p in zip(tops, totals, products):
            w = jnp.exp(t - peak)
            total = total + w * s
            product = product + w * p
        return peak, total, product

    arrived(seven(pr), pr_r)
    arrived(seven(sr), sr_r)
    peak, total, product = merged(
        [sr[k, 0:1] for k in range(NZ)], [sr[k, 1:2] for k in range(NZ)], [pr[k] for k in range(NZ)]
    )
    py[yh] = product
    sy[yh, 0:1] = peak
    sy[yh, 1:2] = total
    send(py.at[yh], py.at[yh], py_s, py_r, partner)
    send(sy.at[yh], sy.at[yh], sy_s, sy_r, partner)

    arrived(seven(lr), lr_r)
    label_part = lr[0].astype(F32)
    for k in range(1, NZ):
        label_part = label_part + lr[k].astype(F32)
    ly[yh] = label_part.astype(BF16)
    send(ly.at[yh], ly.at[yh], ly_s, ly_r, partner)

    arrived(seven(hr), hz_r)
    packed = hr[0].astype(F32)
    for k in range(1, NZ):
        packed = packed + hr[k].astype(F32)
    hproj = jnp.concatenate(
        [packed[0:32], jnp.concatenate([packed[32:48, 0:64], packed[32:48, 64:]], 0)], 1
    )
    h_high = hproj.astype(BF16)
    h_low = (hproj - h_high.astype(F32)).astype(BF16)
    rhs = jnp.concatenate([h_high] * 4 + [h_low] * 4, 0)

    arrived(ts.at[1 - yh], ty_r)
    for k in Z_ORDER:
        o, device = at_z(k)
        for y in range(2):
            send(ts.at[y, o], rt.at[y, z], (rt_s, ru_s)[y], (rt_r, ru_r)[y], device)
    for y in range(2):
        rt[y, z] = ts[y, z]

    arrived(py.at[1 - yh], py_r)
    arrived(sy.at[1 - yh], sy_r)
    peak, total, product = merged(
        [sy[k, 0:1] for k in range(2)], [sy[k, 1:2] for k in range(2)], [py[k] for k in range(2)]
    )
    arrived(ly.at[1 - yh], ly_r)
    rproj = product / total - (ly[0].astype(F32) + ly[1].astype(F32))

    span_of = iota((8, tokens), 1) // SPAN
    high = rproj.astype(BF16).astype(F32)
    low = rproj - high
    lhs = [jnp.where(span_of == s, high, 0.0) for s in range(spans)]
    lhs += [jnp.where(span_of == s, low, 0.0) for s in range(spans)]
    outer = dot_nt(jnp.concatenate(lhs, 0).astype(BF16), rhs)
    outer = (outer[0 : 8 * spans, 128:] + outer[8 * spans :, 0:128]) + outer[0 : 8 * spans, 0:128]
    block = iota((8, 128), 1) // 32
    pair = iota((8, 128), 0) >> 1
    tile = jnp.zeros((8, 128), F32)
    for s in range(spans):
        a = outer[8 * s : 8 * s + 8]
        for jq in range(4):
            shift = (2 * s - 2 * jq) % 8
            moved = pltpu.roll(a, shift, 0) if shift else a
            tile = jnp.where((pair == s) & (block == jq), moved, tile)
    gs[...] = tile.astype(BF16)

    half = 2 * nplace
    me = core * half + yh * nplace + place
    for device in far:
        send(gs, gr.at[me], gr_s, grf_r, device)
    for device in near:
        send(gs, gr.at[me], gr_s, grn_r, device)
    gr[me] = gs[...]

    arrived(gr0.at[pl.ds(0, nplace - 1)], g0_r)
    mine = gr0.at[pl.ds(core * nplace, nplace)]
    send(mine, mine, i_s, i_r, sibling)
    arrived(mine, i_r)
    nrows = ndp * 8
    groups = gr0[...].reshape(nrows, 128).astype(F32)
    member = jnp.where(groups == iota((nrows, 128), 1).astype(F32), 1.0, 0.0)
    member = jnp.transpose(member, (1, 0))[0:GROUPS]
    rr, col = iota((64, nrows), 0), iota((64, nrows), 1)
    a, zz = rr & 7, rr >> 3
    late = (a >= 3).astype(jnp.int32)
    source = 4 * (2 * (2 * zz + yh) + late) + (a - 3 * late)
    span = 4 * (2 * ((col >> 3) & (nplace - 1)) + col // (8 * nplace)) + ((col >> 1) & 3)
    pick = jnp.where((span == source) & (a < 6), 1.0, 0.0)
    cmat[...] = jnp.concatenate([member, pick], 0).astype(BF16)

    sent(hy, hy_s)
    sent(seven(hr), hz_s)
    sent(seven(pr), pr_s)
    sent(seven(sr), sr_s)
    sent(seven(lr), lr_s)
    sent(seven(rt.at[0]), rt_s)
    sent(seven(rt.at[1]), ru_s)
    sent(py.at[0], py_s)
    sent(sy.at[0], sy_s)
    sent(ly.at[0], ly_s)
    sent(rt.at[0], ty_s)
    sent(gr0.at[pl.ds(0, nplace - 1)], g0_s)
    sent(mine, i_s)
    drain()

    for y in range(2):
        arrived(seven(rt.at[y]), (rt_r, ru_r)[y])
    r = iota((256, 256), 0)
    want = ((r >> 2) & 7) * 32 + (r >> 7) * 16 + ((r >> 5) & 3) * 4 + (r & 3)
    perm = jnp.where(iota((256, 256), 1) == want, 1.0, 0.0).astype(BF16)
    for y in range(2):
        tb[y] = dot(perm, rt[y].reshape(256, 128)).astype(BF16).reshape(2, 128, 128)

    arrived(gr.at[pl.ds(0, nplace - 1)], grn_r)
    nearby = gr.at[pl.ds(core * half + yh * nplace, nplace)]
    send(nearby, nearby, fn_s, fn_r, sibling)
    arrived(gr.at[pl.ds(0, nplace)], grf_r)
    distant = gr.at[pl.ds(core * half + (1 - yh) * nplace, nplace)]
    send(distant, distant, ff_s, ff_r, sibling)

    hrows = nplace * 8
    jrow = iota((hrows, 128), 0) & 1

    def scored(c, y):
        grads = gr[pl.ds(c * half + y * nplace, nplace)].reshape(hrows, 128)
        return jnp.where(jrow == 0, dot(grads, tb[y, 0]), dot(grads, tb[y, 1]))

    def split(value):
        one = value.astype(BF16)
        return one, (value - one.astype(F32)).astype(BF16)

    arrived(nearby, fn_r)
    ours = pl.ds(core * hrows, hrows)
    vals[ours, 0:128], vals[ours, 128:256] = split(scored(core, 0) + scored(core, 1))
    here = scored(1 - core, yh)

    arrived(distant, ff_r)

    theirs = pl.ds((1 - core) * hrows, hrows)
    vals[theirs, 0:128], vals[theirs, 128:256] = split(here + scored(1 - core, 1 - yh))
    both_parts = dot(cmat[...], vals[...])
    summed = both_parts[:, 128:] + both_parts[:, 0:128]
    low = summed.astype(BF16)
    for o in range(NZ):
        fs[o, 0:GROUPS] = low[0:GROUPS]
        fs[o, GROUPS:] = low[GROUPS + 8 * o : GROUPS + 8 * o + 8]

    for k in Z_ORDER:
        o, device = at_z(k)
        send(fs.at[o], fsr.at[z], fs_s, fs_r, device)
    fsr[z] = fs[z]

    sent(gr.at[pl.ds(0, half - 1)], gr_s)
    sent(nearby, fn_s)
    sent(distant, ff_s)
    sent(seven(fsr), fs_s)
    drain()

    arrived(seven(fsr), fs_r)

    total = fsr[0].astype(F32)
    for k in range(1, NZ):
        total = total + fsr[k].astype(F32)
    out_s[...] = total[GROUPS : GROUPS + 6]
    out_g[...] = total[0:GROUPS]


def per_device(ndp, logits, labels, hidden, proj_in, proj_out, test_grads, group_ids):
    tokens, width = logits.shape
    any_spec = pl.BlockSpec(memory_space=pl.ANY)
    vmem = pl.BlockSpec(memory_space=pltpu.VMEM)
    dma, V = pltpu.SemaphoreType.DMA, pltpu.VMEM
    row_chunks = (96, 96)
    s, g = pl.pallas_call(
        functools.partial(kernel, ndp, row_chunks),
        name="scores",
        out_shape=(
            pltpu.VMEM((6, 128), F32),
            pltpu.VMEM((GROUPS, 128), F32),
        ),
        in_specs=[any_spec] * 7,
        out_specs=(vmem, vmem),
        scratch_shapes=[
            V((tokens, width), BF16), V((RANK + 16, width), BF16), V((1, tokens), jnp.int32), V((1, 3), jnp.int32),
            V((tokens, 256), BF16), V((RANK, 256), BF16), V((128, 256), BF16),
            V((2, 48, 128), F32), V((2, 48, 128), BF16), V((48, 128), BF16), V((48, 128), BF16), V((NZ, 48, 128), BF16),
            V((NZ, 8, tokens), F32), V((NZ, 8, tokens), F32), V((2, 8, tokens), F32),
            V((2, tokens), F32), V((NZ, 2, tokens), F32), V((2, 2, tokens), F32),
            V((NZ, 8, tokens), BF16), V((NZ, 8, tokens), BF16), V((2, 8, tokens), BF16),
            V((2, NZ, 32, 128), BF16), V((2, NZ, 32, 128), BF16), V((2, 2, 128, 128), BF16),
            V((8, 128), BF16), V((ndp, 8, 128), BF16), V((8, 128), BF16), V((2 * ndp, 8, 128), BF16),
            V((96, ndp * 8), BF16), V((ndp * 8, 256), BF16),
            V((NZ, GROUPS + 8, 128), BF16), V((NZ, GROUPS + 8, 128), BF16),
            dma((6,)), dma((len(row_chunks),)),
            *[dma] * 35, pltpu.SemaphoreType.REGULAR,
        ],
        compiler_params=pltpu.CompilerParams(collective_id=0, has_side_effects=True),
    )(
        logits, labels.reshape(1, tokens), hidden, proj_in.T, proj_out.T, test_grads,
        group_ids.reshape(1, 3),
    )
    return s, g


def solution(mesh):
    in_specs = (
        P("dp", "vocab"),
        P("dp"),
        P("dp", "vocab"),
        P("vocab", None),
        P("vocab", None),
        P("dp", "vocab"),
        P("dp"),
    )
    out_specs = (P("vocab", "dp"), P(None, "dp"))
    return jax.shard_map(
        functools.partial(per_device, mesh.shape["dp"]),
        mesh=mesh, in_specs=in_specs, out_specs=out_specs, check_vma=False,
    )
```
